256 devices in a mesh: dp: 16 (over x, z_lo), fsdp: 16 (over z_hi, y, core).
Axes of the slice: x: 4, y: 4, z: 8 (z_hi: 2, z_lo: 4; z = z_hi * 4 + z_lo), core: 2. Of those that a mesh axis runs over, the one named last changes fastest.
Arguments:
- layer_in: bfloat16 [4096, 16, 5120], P(('dp', 'fsdp')), may hold values from -6 to 6
- norm_gain: float32 [5120], replicated, may hold values from 0.25 to 1.75
- v_weight: bfloat16 [5120, 512], P('fsdp'), may hold values from -0.078125 to 0.078125
- v_bias: float32 [512], replicated, may hold values from -3 to 3
- corpus: int32 [4096], P(('dp', 'fsdp')), may hold values from 0 to 19
- mixture: int32 [20], replicated, may hold values from 1 to 9
- keep_count: int32 [16, 16], P('dp', 'fsdp'), may hold values from 6 to 12, as said below
- keep_seq: int32 [16, 16, 12], P('dp', 'fsdp'), may hold values from -1 to 15, as said below
- keep_dest: int32 [16, 16, 12], P('dp', 'fsdp'), may hold values from -1 to 15, as said below
- value_grad: bfloat16 [16, 16, 16, 16, 512], P('dp', 'fsdp'), may hold values from -6 to 6
Outputs:
- values: bfloat16 [4096, 16, 512], P(('dp', 'fsdp'))
- input_grad: bfloat16 [16, 16, 16, 16, 5120], P('dp', 'fsdp')
- weight_grad: float32 [5120, 512], P('fsdp')
- gain_grad: float32 [5120], replicated
- bias_grad: float32 [512], replicated
The draws below stay inside these ranges and needn't reach their ends.
Inputs may be any that keep to these rules, and one draw needn't show every extreme that they name: `keep_count`: every device keeps at least 6 sequences; some device keeps 12. `keep_seq`: in each row the first keep_count entries are distinct local sequence indices and the rest are -1. `keep_dest`: in each row the first keep_count entries are distinct dp indices and the rest are -1, so one source sends at most one sequence to one destination.
All inputs are finite; a program needn't handle non-finite values.
Results may differ from the reference program's by a relative error of at most 0.005.
Values may be sent and summed in bfloat16 or wider, within the bound.
A program may use at most 128 MiB of HBM per device.

```python
import jax
import jax.numpy as jnp
from jax import lax

D = 5120
KVD = 512
CORPORA = 20
SEQ_DEV = 16
SEQ_LEN = 16
KEEP_MAX = 12
SEQS = 4096
N_DP = 16
N_FSDP = 16


def keep_plan(key):
    base = jax.random.fold_in(key, 11)
    key_count, key_pick, key_seq, key_dest = jax.random.split(base, 4)
    counts = jax.random.randint(key_count, (N_DP, N_FSDP), max(1, KEEP_MAX // 2), KEEP_MAX + 1)
    chosen = jax.random.randint(key_pick, (), 0, N_DP * N_FSDP)
    flat_index = jnp.arange(N_DP)[:, None] * N_FSDP + jnp.arange(N_FSDP)[None, :]
    counts = jnp.where(flat_index == chosen, KEEP_MAX, counts).astype(jnp.int32)
    seq_scores = jax.random.randint(key_seq, (N_DP, N_FSDP, SEQ_DEV), 0, 1 << 20) * SEQ_DEV + jnp.arange(SEQ_DEV)[None, None, :]
    seq_order = jnp.argsort(seq_scores, axis=2, stable=True)[:, :, :KEEP_MAX].astype(jnp.int32)
    dest_scores = jax.random.randint(key_dest, (N_DP, N_FSDP, N_DP), 0, 1 << 20) * N_DP + jnp.arange(N_DP)[None, None, :]
    dest_order = jnp.argsort(dest_scores, axis=2, stable=True)[:, :, :KEEP_MAX].astype(jnp.int32)
    valid = jnp.arange(KEEP_MAX)[None, None, :] < counts[:, :, None]
    return (counts, jnp.where(valid, seq_order, -1).astype(jnp.int32), jnp.where(valid, dest_order, -1).astype(jnp.int32))


def draw_keep_count(key, part):
    return keep_plan(key)[0]


def draw_keep_seq(key, part):
    return keep_plan(key)[1]


def draw_keep_dest(key, part):
    return keep_plan(key)[2]


def place_ends(result, rng, low, largest):
    dims = result.shape
    index_at = [jax.random.randint(jax.random.fold_in(rng, axis), (), 0, dims[axis]) for axis in range(len(dims))]
    result = result.at[tuple(index_at)].set(low)
    longest = dims.index(max(dims))
    index_at[longest] = (index_at[longest] + 1) % dims[longest]
    return result.at[tuple(index_at)].set(largest)


def steps_of(key, shape, cuts, low, top_value):
    factor_of = 1.0
    for dim, shards_of in cuts:
        steps = jax.random.uniform(jax.random.fold_in(jax.random.fold_in(key, 6), dim), (shards_of,), jnp.float32, low / len(cuts), top_value / len(cuts))
        factor_of = factor_of * jnp.repeat(jnp.exp(steps), shape[dim] // shards_of).reshape((-1,) + (1,) * (len(shape) - 1 - dim))
    return factor_of


def normal_values(stream_key, dims, spread, limit, cuts=(), held_as=jnp.bfloat16):
    loudness = steps_of(stream_key, dims, cuts, -0.22, 0.18) if cuts else 1.0
    values = jax.random.normal(stream_key, dims, jnp.float32) * spread * loudness
    return jnp.minimum(jnp.maximum(values, -limit), limit).astype(held_as)


def setup_inputs(seed: int = 0) -> dict:
    streams_of = jax.random.split(jax.random.key(seed), 11)
    layer_in = normal_values(streams_of[0], (SEQS, SEQ_LEN, D), 1.0, 6.0, ((0, 256),))
    norm_gain = jnp.clip(1.0 + 0.15 * jax.random.normal(streams_of[1], (D,), jnp.float32), 0.25, 1.75)
    v_weight = normal_values(streams_of[2], (D, KVD), D ** -0.5, 0.078125, ((0, 16),))
    v_bias = normal_values(streams_of[3], (KVD,), 0.5, 3.0, (), jnp.float32)
    corpus = place_ends(jax.random.randint(streams_of[4], (SEQS,), 0, CORPORA), jax.random.fold_in(streams_of[4], 1), 0, CORPORA - 1).astype(jnp.int32)
    mixture = place_ends(jax.random.randint(streams_of[5], (CORPORA,), 1, 10), jax.random.fold_in(streams_of[5], 1), 1, 9).astype(jnp.int32)
    keep_count = draw_keep_count(jax.random.fold_in(streams_of[10], 71), 0)
    keep_seq = draw_keep_seq(jax.random.fold_in(streams_of[10], 71), 0)
    keep_dest = draw_keep_dest(jax.random.fold_in(streams_of[10], 71), 0)
    value_grad = normal_values(streams_of[9], (N_DP, N_FSDP, N_DP, SEQ_LEN, KVD), 1.0, 6.0, ((0, 16), (1, 16)))
    return {"layer_in": layer_in, "norm_gain": norm_gain, "v_weight": v_weight, "v_bias": v_bias, "corpus": corpus, "mixture": mixture, "keep_count": keep_count, "keep_seq": keep_seq, "keep_dest": keep_dest, "value_grad": value_grad}


EPSILON = 1e-06

def normalize(layer_rows, norm_gain):
    widened = layer_rows.astype(jnp.float32)
    inverse_rms = lax.rsqrt(lax.optimization_barrier(jnp.mean(widened * widened, axis=-1, keepdims=True)) + EPSILON)
    normed = (widened * inverse_rms * norm_gain).astype(jnp.bfloat16)
    return (normed, widened, inverse_rms)

def slot_table(corpus, mixture, keep_count, keep_seq, keep_dest):
    valid = jnp.arange(KEEP_MAX)[None, None, :] < keep_count[:, :, None]
    hits = (keep_dest[:, :, :, None] == jnp.arange(N_DP)[None, None, None, :]) & valid[:, :, :, None]
    device_base = (jnp.arange(N_DP)[:, None] * N_FSDP + jnp.arange(N_FSDP)[None, :]) * SEQ_DEV
    global_seq = device_base[:, :, None] + keep_seq
    slot_seq = lax.optimization_barrier(jnp.sum(jnp.where(hits, global_seq[:, :, :, None], 0), axis=2))
    slot_seq = jnp.transpose(slot_seq, (2, 1, 0)).astype(jnp.int32)
    is_live = jnp.transpose(jnp.any(hits, axis=2), (2, 1, 0))
    corpus_mix = mixture[corpus]
    slot_mix = jnp.where(is_live, corpus_mix[slot_seq], 0).astype(jnp.float32)
    kept_total = jnp.sum(slot_mix)
    kept_number = jnp.sum(is_live.astype(jnp.float32))
    slot_scale = slot_mix * kept_number / kept_total
    return (slot_seq, is_live, slot_scale)

def reference(layer_in, norm_gain, v_weight, v_bias, corpus, mixture, keep_count, keep_seq, keep_dest, value_grad):

    def forward_one(block):
        normed, _, _ = normalize(block, norm_gain)
        return (jnp.dot(normed, v_weight, preferred_element_type=jnp.float32) + v_bias).astype(jnp.bfloat16)
    blocks = layer_in.reshape(SEQS // SEQ_DEV, SEQ_DEV * SEQ_LEN, D)
    values = lax.map(forward_one, blocks).reshape(SEQS, SEQ_LEN, KVD)
    slot_seq, is_live, slot_scale = slot_table(corpus, mixture, keep_count, keep_seq, keep_dest)
    slot_seq = slot_seq.reshape(N_DP * N_FSDP, N_DP)
    is_live = is_live.reshape(N_DP * N_FSDP, N_DP)
    slot_scale = slot_scale.reshape(N_DP * N_FSDP, N_DP)
    grads_in = value_grad.reshape(N_DP * N_FSDP, N_DP, SEQ_LEN, KVD)

    def backward_one(carry, dest_index):
        weight_acc, gain_acc, bias_acc = carry
        picked = jnp.take(layer_in, slot_seq[dest_index], axis=0)
        picked = jnp.where(is_live[dest_index][:, None, None], picked, jnp.zeros_like(picked))
        normed, widened, inverse_rms = normalize(picked, norm_gain)
        scaled = (grads_in[dest_index].astype(jnp.float32) * slot_scale[dest_index][:, None, None]).astype(jnp.bfloat16)
        flat_normed = normed.reshape(-1, D)
        flat_scaled = scaled.reshape(-1, KVD)
        weight_acc = weight_acc + jnp.dot(flat_normed.T, flat_scaled, preferred_element_type=jnp.float32)
        bias_acc = bias_acc + lax.optimization_barrier(jnp.sum(flat_scaled.astype(jnp.float32), axis=0))
        normed_grad = jnp.dot(flat_scaled, v_weight.T, preferred_element_type=jnp.float32).reshape(widened.shape)
        gain_acc = gain_acc + lax.optimization_barrier(jnp.sum(normed_grad * widened * inverse_rms, axis=(0, 1)))
        gained = normed_grad * norm_gain
        input_grad = inverse_rms * gained - widened * inverse_rms ** 3 * lax.optimization_barrier(jnp.mean(gained * widened, axis=-1, keepdims=True))
        return ((weight_acc, gain_acc, bias_acc), input_grad.astype(jnp.bfloat16))
    start = (jnp.zeros((D, KVD), jnp.float32), jnp.zeros((D,), jnp.float32), jnp.zeros((KVD,), jnp.float32))
    (weight_grad, gain_grad, bias_grad), input_grad = lax.scan(backward_one, start, jnp.arange(N_DP * N_FSDP))
    input_grad = input_grad.reshape(N_DP, N_FSDP, N_DP, SEQ_LEN, D)
    return (values, input_grad, weight_grad, gain_grad, bias_grad)
```

```python
import jax
import jax.numpy as jnp
from jax import lax
from jax.experimental import pallas as pl
from jax.experimental.pallas import tpu as pltpu
from jax.sharding import PartitionSpec as P

EPSILON = 1e-06
MESH = pl.DeviceIdType.MESH
F32 = jnp.float32
BF16 = jnp.bfloat16

NX, NZ, NY, NC = 4, 4, 4, 2
NDP, NF = 16, 16
TOK = 16
D, V = 5120, 512
Q = 8
QW = D // Q
SH = D // NF


def put(src, dst, send, recv, device):
    return pltpu.make_async_remote_copy(
        src_ref=src, dst_ref=dst, send_sem=send, recv_sem=recv, device_id=device, device_id_type=MESH
    )


def lanes(q):
    return pl.ds(pl.multiple_of(q * QW, 128), QW)


def kernel(
    x_ref, gain_ref, w_ref, bias_ref, vg_ref, corpus_ref, mixture_ref, count_ref, seq_ref, dest_ref,
    values_ref, igrad_ref, m_ref, gg_out, stat_ref,
    xs, xr, mixs, mixr, nf, rms, a3, ap, vgr, vgp, wf, acc, ng,
    ms, mr, mown, mxs, mxr, mx, mzs, mzr, ags, agr, ggs, ggr, st, sty, stx, stz, stc,
    vg_s, vg_r, x_s, x_r, mix_s, mix_r, w_s, w_r, ap_s, vgp_s, my_s, my_r, mx_s, mx_r, mz_s, mz_r,
    ag_s, ag_r, gg_s, gg_r, sty_s, sty_r, stx_s, stx_r, stz_s, stz_r, stc_s, loc,
):
    me = lax.axis_index("dp")
    f = lax.axis_index("fsdp")
    x, zl = me // NZ, me % NZ
    zh, y, c = f // 8, (f // 2) % NY, f % 2
    z = zh * 4 + zl

    def at(x_, z_, y_, c_):
        return (x_ * NZ + z_ % 4, (z_ // 4) * 8 + y_ * 2 + c_)

    partner = (me, zh * 8 + y * 2 + 1 - c)

    bar = pltpu.get_barrier_semaphore()
    greeted = 0
    for k in range(1, 16):
        other = (me + k) % 16
        for dev in ((other, f), (other, partner[1]), (me, (f + k) % 16)):
            pl.semaphore_signal(bar, inc=1, device_id=dev, device_id_type=MESH)
            greeted += 1
    for k in range(1, 4):
        pl.semaphore_signal(
            bar, inc=1, device_id=(x * NZ + (zl + k) % 4, (1 - zh) * 8 + y * 2 + c), device_id_type=MESH
        )
        greeted += 1

    def slot(d):
        chosen, live = jnp.int32(0), jnp.int32(0)
        for j in range(dest_ref.shape[0]):
            hit = (dest_ref[j] == d) & (j < count_ref[0])
            chosen = jnp.where(hit, seq_ref[j], chosen)
            live = jnp.where(hit, 1, live)
        mix = mixture_ref[corpus_ref[chosen]] * live
        return chosen, live, mix.astype(F32)

    def gather(d, carry):
        total, number = carry
        chosen, live, mix = slot(d)
        xs[d] = x_ref[chosen]
        mixs[d] = jnp.broadcast_to(mix, (1, 128))
        return total + mix, number + live.astype(F32)

    kept_total, kept_number = lax.fori_loop(0, 16, gather, (jnp.float32(0), jnp.float32(0)))

    pl.semaphore_wait(bar, greeted)

    def vg_put(k):
        d = (me + k) % 16
        return put(vg_ref.at[d], vgr.at[me], vg_s.at[k], vg_r.at[me], (d, f))

    def mix_put(k):
        d = (me + k) % 16
        return put(mixs.at[d], mixr.at[me], mix_s.at[k], mix_r.at[me], (d, f))

    def x_put(k):
        d = (me + k) % 16
        return put(xs.at[d], xr.at[me], x_s.at[k], x_r.at[me], (d, f))

    def w_put(slot_, sem, dev, own=False):
        return put(w_ref if own else wf.at[slot_], wf.at[slot_], w_s.at[sem], w_r.at[slot_], dev)

    def each(start, stop, fn):
        def step(i, carry):
            fn(i)
            return carry

        lax.fori_loop(start, stop, step, 0)

    each(1, 16, lambda k: vg_put(k).start())
    edge = (zl == 0) | (zl == 3)
    far = (1 - zh) * 4 + jnp.where(zl == 0, 3, 0)
    near = (1 - zh) * 4 + jnp.where(zl == 0, 2, 1)

    @pl.when(edge)
    def _():
        w_put(f, 4, at(x, far, y, c), True).start()
        w_put(f, 5, at(x, near, y, c), True).start()

    for k in (2, 1, 3):
        w_put(f, k, at(x, z, (y + k) % 4, c), True).start()
    w_put(f, 0, partner, True).start()
    each(1, 16, lambda k: mix_put(k).start())
    each(1, 16, lambda k: x_put(k).start())
    own_w = pltpu.make_async_copy(w_ref, wf.at[f], loc.at[0])
    own_x = pltpu.make_async_copy(xs.at[me], xr.at[me], loc.at[1])
    own_vg = pltpu.make_async_copy(vg_ref.at[me], vgr.at[me], loc.at[2])
    own_mix = pltpu.make_async_copy(mixs.at[me], mixr.at[me], loc.at[3])
    for cp in (own_w, own_x, own_vg, own_mix):
        cp.start()

    def norm(i):
        total = jnp.zeros((TOK, 128), F32)
        for q in range(Q):
            part = x_ref[i, :, q * QW : (q + 1) * QW].astype(F32)
            part = part * part
            for b in range(QW // 128):
                total = total + part[:, b * 128 : (b + 1) * 128]
        inverse = lax.rsqrt(jnp.sum(total, axis=1, keepdims=True) / D + EPSILON)
        rms[i] = jnp.broadcast_to(inverse, (TOK, 128))
        for q in range(Q):
            cols = slice(q * QW, (q + 1) * QW)
            nf[i, :, cols] = (x_ref[i, :, cols].astype(F32) * inverse * gain_ref[:, cols]).astype(BF16)

    each(0, 16, norm)

    def weigh(d):
        chosen, _, mix = slot(d)
        factor = rms[chosen][:, :1] * mix
        for q in range(Q):
            a3[q, d] = (xs[d, :, q * QW : (q + 1) * QW].astype(F32) * factor).astype(BF16)

    each(0, 16, weigh)
    ap_put = put(a3.at[pl.ds((1 - c) * 4, 4)], ap, ap_s.at[0], ap_s.at[1], partner)
    ap_put.start()

    own_vg.wait()
    each(1, 16, lambda k: put(vg_ref.at[0], vgr.at[(me + 16 - k) % 16], vg_s.at[k], vg_r.at[(me + 16 - k) % 16], partner).wait_recv())
    vgp_put = put(vgr, vgp, vgp_s.at[0], vgp_s.at[1], partner)
    vgp_put.start()

    def add_bias(d, total):
        return total + vgr[d].astype(F32) * mixs[d][:, :1]

    bias_rows = lax.fori_loop(0, 16, add_bias, jnp.zeros((TOK, V), F32))
    row = lax.broadcasted_iota(jnp.int32, (8, V), 0)
    mine = jnp.where(
        row == 0, jnp.sum(bias_rows, axis=0, keepdims=True),
        jnp.where(row == 1, kept_total, jnp.where(row == 2, kept_number, 0.0)),
    )
    st[0] = mine
    sty[y] = mine
    st_y = [put(st.at[0], sty.at[y], sty_s.at[k], sty_r.at[y], at(x, z, (y + k) % 4, c)) for k in (1, 2, 3)]
    for cp in st_y:
        cp.start()

    ap_put.wait_recv()
    vgp_put.wait_recv()

    def share(yq, store):
        for b in range(QW // 128):
            cols = slice(b * 128, (b + 1) * 128)
            both = (((0,), (0,)), ((), ()))
            left = a3[c * 4 + yq, :, :, cols].reshape(16 * TOK, 128)
            right = ap[yq, :, :, cols].reshape(16 * TOK, 128)
            part = lax.dot_general(left, vgr[...].reshape(16 * TOK, V), both, preferred_element_type=F32)
            part += lax.dot_general(right, vgp[...].reshape(16 * TOK, V), both, preferred_element_type=F32)
            store(cols, part)

    m_y = []
    for k in (2, 1, 3):
        yq = (y + k) % 4

        def to_send(cols, part, k=k):
            ms[k - 1, cols, :] = part.astype(BF16)

        share(yq, to_send)
        cp = put(ms.at[k - 1], mr.at[k - 1], my_s.at[k], my_r.at[k], at(x, z, yq, c))
        cp.start()
        m_y.append(cp)

    def to_own(cols, part):
        mown[cols, :] = part

    share(y, to_own)

    oz = (1 - zh) * 8 + c
    w_in = lambda slot_: put(w_ref, wf.at[slot_], w_s.at[0], w_r.at[slot_], partner)
    w_in(oz + y * 2).wait_recv()
    for k in (2, 1, 3):
        w_put(oz + y * 2, 5 + k + (k > 0), at(x, z, (y + k) % 4, c)).start()
    w_put(oz + y * 2, 10, partner).start()
    for k in (1, 3, 2):
        s = zh * 8 + ((y + k) % 4) * 2 + c
        w_in(s).wait_recv()
        w_put(s, 10 + k, partner).start()

    for k in (1, 2, 3):
        put(st.at[0], sty.at[(y + k) % 4], sty_s.at[k], sty_r.at[(y + k) % 4], partner).wait_recv()
    mine = ((sty[0] + sty[1]) + sty[2]) + sty[3]
    st[1] = mine
    stx[x] = mine
    st_x = [put(st.at[1], stx.at[x], stx_s.at[k], stx_r.at[x], at((x + k) % 4, z, y, c)) for k in (1, 2, 3)]
    for cp in st_x:
        cp.start()

    own_w.wait()
    acc[...] = jnp.zeros_like(acc)
    vg_all = vg_ref

    def block(q):
        rows = wf[pl.ds(q * 2, 2)].reshape(QW, V)
        acc[...] += jnp.dot(nf[:, :, lanes(q)].reshape(16 * TOK, QW), rows, preferred_element_type=F32)
        grad = lax.dot_general(
            vg_all[...].reshape(16 * TOK, V), rows, (((1,), (1,)), ((), ())), preferred_element_type=F32
        )
        ng[:, :, lanes(q)] = grad.reshape(16, TOK, QW)

    def first_blocks(k):
        yq = (y + k) % 4
        w_in(zh * 8 + yq * 2 + 1 - c).wait_recv()
        block(zh * 4 + yq)

    each(0, 4, first_blocks)

    for k in (1, 2, 3):
        put(st.at[0], stx.at[(x + k) % 4], stx_s.at[k], stx_r.at[(x + k) % 4], partner).wait_recv()
    mine = ((stx[0] + stx[1]) + stx[2]) + stx[3]
    st[2] = mine
    stz[z] = mine
    st_z = [put(st.at[2], stz.at[z], stz_s.at[k], stz_r.at[z], at(x, (z + k) % 8, y, c)) for k in range(1, 8)]
    for cp in st_z:
        cp.start()

    for k in (1, 2, 3):
        put(ms.at[0], mr.at[k - 1], my_s.at[k], my_r.at[k], partner).wait_recv()
    for b in range(QW // 128):
        cols = slice(b * 128, (b + 1) * 128)
        total = mown[cols, :] + mr[0, cols, :].astype(F32) + mr[1, cols, :].astype(F32) + mr[2, cols, :].astype(F32)
        mown[cols, :] = total
        mxs[cols, :] = total.astype(BF16)
    m_x = []
    for k in (2, 1, 3):
        xq = (x + k) % 4
        cp = put(
            mxs.at[pl.ds(pl.multiple_of(xq * 160, 32), 160)], mxr.at[k - 1], mx_s.at[k], mx_r.at[k], at(xq, z, y, c)
        )
        cp.start()
        m_x.append(cp)

    for k in (1, 3, 2):
        s = oz + ((y + k) % 4) * 2
        w_in(s).wait_recv()
        w_put(s, 13 + k - (k == 0), partner).start()

    for k in (1, 2, 3):
        put(mxs.at[pl.ds(0, 160)], mxr.at[k - 1], mx_s.at[k], mx_r.at[k], partner).wait_recv()
    mx[...] = (
        mown[pl.ds(pl.multiple_of(x * 160, 32), 160), :]
        + mxr[0].astype(F32) + mxr[1].astype(F32) + mxr[2].astype(F32)
    )
    for b in range(4):
        mzs[b] = mx[b * 40 : (b + 1) * 40, :].astype(BF16)

    def z_put(k):
        zq = (z + k) % 8
        return put(mzs.at[zq % 4], mzr.at[z], mz_s.at[k], mz_r.at[z], at(x, zq, y, c))

    for k in range(1, 8):
        @pl.when((z + k) % 8 // 4 == c)
        def _(k=k):
            z_put(k).start()

    def last_blocks(k):
        yq = (y + k) % 4
        w_in((1 - zh) * 8 + yq * 2 + 1 - c).wait_recv()
        block((1 - zh) * 4 + yq)

    each(0, 4, last_blocks)
    values_ref[...] = (acc[...] + bias_ref[...]).astype(BF16)

    sums_here = zh == c
    to_core = x // 2
    place = (x % 2) * 4 + zl

    def ag_put(k):
        return put(ags, agr.at[place], ag_s.at[k], ag_r.at[place], ((me + k) % 16, zh * 8 + y * 2 + to_core))

    @pl.when(sums_here)
    def _():
        mzr[z] = mzs[zl]
        for k in range(1, 8):
            zq = (z + k) % 8
            put(mzs.at[0], mzr.at[zq], mz_s.at[k], mz_r.at[zq], partner).wait_recv()
        total = mzr[0].astype(F32)
        for b in range(1, 8):
            total += mzr[b].astype(F32)
        ags[...] = total.astype(BF16)
        each(1, 16, lambda k: ag_put(k).start())

        @pl.when(to_core == c)
        def _():
            agr[place] = ags[...]

        @pl.when(to_core != c)
        def _():
            ag_put(0).start()

    for k in range(1, 8):
        zq = (z + k) % 8
        put(st.at[0], stz.at[zq], stz_s.at[k], stz_r.at[zq], partner).wait_recv()
    total = stz[0]
    for b in range(1, 8):
        total = total + stz[b]
    st[3] = total
    st_c = put(st.at[3], stc, stc_s.at[0], stc_s.at[1], partner)
    st_c.start()
    st_c.wait_recv()
    total = total + stc[...]
    stat_ref[...] = total
    ratio = total[2:3, 0:1] / total[1:2, 0:1]

    own_x.wait()
    own_mix.wait()

    def slot_grad(s):
        squares = jnp.zeros((TOK, 128), F32)
        products = jnp.zeros((TOK, 128), F32)
        for q in range(Q):
            cols = slice(q * QW, (q + 1) * QW)
            rows = xr[s, :, cols].astype(F32)
            both = ng[s, :, cols] * gain_ref[:, cols] * rows
            rows = rows * rows
            for b in range(QW // 128):
                squares = squares + rows[:, b * 128 : (b + 1) * 128]
                products = products + both[:, b * 128 : (b + 1) * 128]
        inverse = lax.rsqrt(jnp.sum(squares, axis=1, keepdims=True) / D + EPSILON)
        mean = jnp.sum(products, axis=1, keepdims=True) / D
        scale = ratio * mixr[s][:, :1]
        left = inverse * scale
        right = inverse * inverse * inverse * mean * scale
        for q in range(Q):
            cols = slice(q * QW, (q + 1) * QW)
            rows = xr[s, :, cols].astype(F32)
            igrad_ref[s, :, cols] = (left * (ng[s, :, cols] * gain_ref[:, cols]) - rows * right).astype(BF16)

    slot_grad(me)

    def take(k):
        s = (me + 16 - k) % 16
        put(mixs.at[0], mixr.at[s], mix_s.at[k], mix_r.at[s], partner).wait_recv()
        put(xs.at[0], xr.at[s], x_s.at[k], x_r.at[s], partner).wait_recv()
        slot_grad(s)

    each(1, 16, take)

    for xq in range(2):
        for zq in range(4):
            source = xq * 4 + zq
            here = sums_here & (to_core == c) & (place == source)

            @pl.when(jnp.logical_not(here))
            def _(source=source):
                put(ags, agr.at[source], ag_s.at[0], ag_r.at[source], partner).wait_recv()

    part = []
    for b in range(8):
        rows = agr[b].astype(F32)
        m_ref[b * 40 : (b + 1) * 40, :] = rows
        rows = rows * w_ref[b * 40 : (b + 1) * 40, :].astype(F32)
        part.append(rows[:, :128] + rows[:, 128:256] + rows[:, 256:384] + rows[:, 384:])
    part = jnp.concatenate(part, axis=0)
    gains = lax.dot_general(
        jnp.ones((8, 128), F32), part, (((1,), (1,)), ((), ())),
        precision=lax.Precision.HIGHEST, preferred_element_type=F32,
    )
    ggs[...] = gains[:1]
    ggr[f] = gains[:1]

    def gg_put(k):
        return put(ggs, ggr.at[f], gg_s.at[k], gg_r.at[f], (me, (f + k) % 16))

    each(1, 16, lambda k: gg_put(k).start())

    def gg_wait(k):
        s = (f + k) % 16
        put(ggs, ggr.at[s], gg_s.at[k], gg_r.at[s], partner).wait_recv()

    each(1, 16, gg_wait)
    gg_out[...] = ggr[...]

    def sent(k):
        vg_put(k).wait_send()
        mix_put(k).wait_send()
        x_put(k).wait_send()
        gg_put(k).wait_send()

    each(1, 16, sent)

    @pl.when(edge)
    def _():
        w_put(f, 4, partner).wait_send()
        w_put(f, 5, partner).wait_send()

    for sem in (0, 1, 2, 3, 7, 8, 9, 10, 11, 12, 13, 14, 15, 16):
        w_put(f, sem, partner).wait_send()
    for cp in [ap_put, vgp_put, st_c] + st_y + st_x + st_z + m_y + m_x:
        cp.wait_send()
    for k in range(1, 8):
        @pl.when((z + k) % 8 // 4 == c)
        def _(k=k):
            z_put(k).wait_send()

    @pl.when(sums_here)
    def _():
        each(1, 16, lambda k: ag_put(k).wait_send())

        @pl.when(to_core != c)
        def _():
            ag_put(0).wait_send()


def body(
    layer_in, norm_gain, v_weight, v_bias, corpus, mixture, keep_count, keep_seq, keep_dest, value_grad
):
    vmem = pl.BlockSpec(memory_space=pltpu.VMEM)
    smem = pl.BlockSpec(memory_space=pltpu.SMEM)
    dma = pltpu.SemaphoreType.DMA
    values, input_grad, m_rows, gains, stats = pl.pallas_call(
        kernel,
        out_shape=(
            jax.ShapeDtypeStruct((16 * TOK, V), BF16),
            jax.ShapeDtypeStruct((16, TOK, D), BF16),
            jax.ShapeDtypeStruct((SH, V), F32),
            jax.ShapeDtypeStruct((NF, 1, SH), F32),
            jax.ShapeDtypeStruct((8, V), F32),
        ),
        in_specs=[vmem] * 5 + [smem] * 5,
        out_specs=[vmem] * 5,
        scratch_shapes=[
            pltpu.VMEM((16, TOK, D), BF16),
            pltpu.VMEM((16, TOK, D), BF16),
            pltpu.VMEM((16, 1, 128), F32),
            pltpu.VMEM((16, 1, 128), F32),
            pltpu.VMEM((16, TOK, D), BF16),
            pltpu.VMEM((16, TOK, 128), F32),
            pltpu.VMEM((Q, 16, TOK, QW), BF16),
            pltpu.VMEM((4, 16, TOK, QW), BF16),
            pltpu.VMEM((16, TOK, V), BF16),
            pltpu.VMEM((16, TOK, V), BF16),
            pltpu.VMEM((NF, SH, V), BF16),
            pltpu.VMEM((16 * TOK, V), F32),
            pltpu.VMEM((16, TOK, D), F32),
            pltpu.VMEM((3, QW, V), BF16),
            pltpu.VMEM((3, QW, V), BF16),
            pltpu.VMEM((QW, V), F32),
            pltpu.VMEM((QW, V), BF16),
            pltpu.VMEM((3, QW // 4, V), BF16),
            pltpu.VMEM((QW // 4, V), F32),
            pltpu.VMEM((4, QW // 16, V), BF16),
            pltpu.VMEM((8, QW // 16, V), BF16),
            pltpu.VMEM((QW // 16, V), BF16),
            pltpu.VMEM((8, QW // 16, V), BF16),
            pltpu.VMEM((1, SH), F32),
            pltpu.VMEM((NF, 1, SH), F32),
            pltpu.VMEM((4, 8, V), F32),
            pltpu.VMEM((4, 8, V), F32),
            pltpu.VMEM((4, 8, V), F32),
            pltpu.VMEM((8, 8, V), F32),
            pltpu.VMEM((8, V), F32),
            dma((16,)), dma((16,)), dma((16,)), dma((16,)), dma((16,)), dma((16,)),
            dma((17,)), dma((16,)), dma((2,)), dma((2,)),
            dma((4,)), dma((4,)), dma((4,)), dma((4,)), dma((8,)), dma((8,)),
            dma((16,)), dma((8,)), dma((16,)), dma((16,)),
            dma((4,)), dma((4,)), dma((4,)), dma((4,)), dma((8,)), dma((8,)), dma((2,)), dma((4,)),
        ],
        compiler_params=pltpu.CompilerParams(
            collective_id=0, has_side_effects=True, vmem_limit_bytes=60 * 1024 * 1024
        ),
        name="step",
    )(
        layer_in, norm_gain[None, :], v_weight, v_bias[None, :], value_grad[0, 0],
        corpus, mixture, keep_count[0], keep_seq[0, 0], keep_dest[0, 0],
    )
    ratio = stats[2, 0] / stats[1, 0]
    first = lax.axis_index("fsdp") * SH
    own_gain = lax.dynamic_slice(norm_gain, (first,), (SH,))
    weight_grad = m_rows * (own_gain * ratio)[:, None]
    gain_grad = gains.reshape(D) * ratio
    bias_grad = stats[0] * ratio
    return (
        values.reshape(16, TOK, V), input_grad[None, None], weight_grad, gain_grad, bias_grad,
    )


def solution(mesh):
    return jax.shard_map(
        body,
        mesh=mesh,
        in_specs=(
            P(("dp", "fsdp"), None, None),
            P(),
            P("fsdp", None),
            P(),
            P(("dp", "fsdp")),
            P(),
            P("dp", "fsdp"),
            P("dp", "fsdp", None),
            P("dp", "fsdp", None),
            P("dp", "fsdp", None, None, None),
        ),
        out_specs=(
            P(("dp", "fsdp"), None, None),
            P("dp", "fsdp", None, None, None),
            P("fsdp", None),
            P(),
            P(),
        ),
        check_vma=False,
    )
```

```python
import jax
import jax.numpy as jnp
from jax import lax
from jax.experimental import pallas as pl
from jax.experimental.pallas import tpu as pltpu
from jax.sharding import PartitionSpec as P

EPSILON = 1e-06
MESH = pl.DeviceIdType.MESH
F32 = jnp.float32
BF16 = jnp.bfloat16

NX, NZ, NY, NC = 4, 4, 4, 2
NDP, NF = 16, 16
TOK = 16
D, V = 5120, 512
Q = 8
QW = D // Q
SH = D // NF


def put(src, dst, send, recv, device):
    return pltpu.make_async_remote_copy(
        src_ref=src, dst_ref=dst, send_sem=send, recv_sem=recv, device_id=device, device_id_type=MESH
    )


def lanes(q):
    return pl.ds(pl.multiple_of(q * QW, 128), QW)


def kernel(
    x_hbm, gain_hbm, w_hbm, bias_hbm, vg_hbm, corpus_hbm, mixture_hbm, count_hbm, seq_hbm, dest_hbm,
    values_ref, igrad_ref, wgrad_ref, ggrad_ref, bgrad_ref,
    x_ref, gain_ref, w_ref, bias_ref, vg_ref, corpus_ref, mixture_ref, count_ref, seq_ref, dest_ref,
    xs, xr, mixs, mixr, nf, a3, ap, vgr, vgp, wf, acc, ng,
    ms, mr, mown, mxs, mxr, mx, mzs, mzr, ags, agr, gs, gx, gz, gq, st, sty, stx, stz, stc,
    vg_s, vg_r, x_s, x_r, mix_s, mix_r, w_s, w_r, ap_s, vgp_s, my_s, my_r, mx_s, mx_r, mz_s, mz_r,
    ag_s, ag_r, gx_s, gx_r, gz_s, gz_r, gq_s, gq_r, sty_s, sty_r, stx_s, stx_r, stz_s, stz_r, stc_s, loc,
):
    me = lax.axis_index("dp")
    f = lax.axis_index("fsdp")
    x, zl = me // NZ, me % NZ
    zh, y, c = f // 8, (f // 2) % NY, f % 2
    z = zh * 4 + zl

    def at(x_, z_, y_, c_):
        return (x_ * NZ + z_ % 4, (z_ // 4) * 8 + y_ * 2 + c_)

    partner = (me, zh * 8 + y * 2 + 1 - c)

    moves = [
        pltpu.make_async_copy(src, dst, loc.at[4 + i])
        for i, (src, dst) in enumerate((
            (corpus_hbm, corpus_ref), (mixture_hbm, mixture_ref), (count_hbm, count_ref), (seq_hbm, seq_ref),
            (dest_hbm, dest_ref), (x_hbm, x_ref), (vg_hbm, vg_ref), (w_hbm, w_ref), (gain_hbm, gain_ref),
            (bias_hbm, bias_ref),
        ))
    ]
    for cp in moves:
        cp.start()

    bar = pltpu.get_barrier_semaphore()
    greeted = 0
    for k in range(1, 16):
        other = (me + k) % 16
        for dev in ((other, f), (other, partner[1])):
            pl.semaphore_signal(bar, inc=1, device_id=dev, device_id_type=MESH)
            greeted += 1
    for k in range(1, 8):
        pl.semaphore_signal(bar, inc=1, device_id=(me, zh * 8 + (f + k) % 8), device_id_type=MESH)
        greeted += 1
    for k in range(4):
        pl.semaphore_signal(
            bar, inc=1, device_id=(x * NZ + k, (1 - zh) * 8 + y * 2 + c), device_id_type=MESH
        )
        greeted += 1
    for cp in moves[:6]:
        cp.wait()

    def slot(d):
        chosen, live = jnp.int32(0), jnp.int32(0)
        for j in range(dest_ref.shape[0]):
            hit = (dest_ref[j] == d) & (j < count_ref[0])
            chosen = jnp.where(hit, seq_ref[j], chosen)
            live = jnp.where(hit, 1, live)
        mix = mixture_ref[corpus_ref[chosen]] * live
        return chosen, live, mix.astype(F32)

    def gather(d, carry):
        total, number = carry
        chosen, live, mix = slot(d)
        xs[d] = x_ref[chosen]
        mixs[d] = jnp.broadcast_to(mix, (1, 128))
        return total + mix, number + live.astype(F32)

    kept_total, kept_number = lax.fori_loop(0, 16, gather, (jnp.float32(0), jnp.float32(0)))

    for cp in moves[6:]:
        cp.wait()
    pl.semaphore_wait(bar, greeted)

    def vg_put(k):
        d = (me + k) % 16
        return put(vg_ref.at[d], vgr.at[me], vg_s.at[k], vg_r.at[me], (d, f))

    def mix_put(k):
        d = (me + k) % 16
        return put(mixs.at[d], mixr.at[me], mix_s.at[k], mix_r.at[me], (d, f))

    def x_put(k):
        d = (me + k) % 16
        return put(xs.at[d], xr.at[me], x_s.at[k], x_r.at[me], (d, f))

    def w_put(slot_, sem, dev, own=False):
        return put(w_ref if own else wf.at[slot_], wf.at[slot_], w_s.at[sem], w_r.at[slot_], dev)

    def each(start, stop, fn):
        def step(i, carry):
            fn(i)
            return carry

        lax.fori_loop(start, stop, step, 0)

    each(1, 16, lambda k: vg_put(k).start())
    edge = (zl == 0) | (zl == 3)
    far = (1 - zh) * 4 + jnp.where(zl == 0, 3, 0)
    near = (1 - zh) * 4 + jnp.where(zl == 0, 2, 1)

    @pl.when(edge)
    def _():
        w_put(f, 4, at(x, far, y, c), True).start()
        w_put(f, 5, at(x, near, y, c), True).start()

    for k in (2, 1, 3):
        w_put(f, k, at(x, z, (y + k) % 4, c), True).start()
    w_put(f, 0, partner, True).start()
    each(1, 16, lambda k: mix_put(k).start())
    each(1, 16, lambda k: x_put(k).start())
    own_w = pltpu.make_async_copy(w_ref, wf.at[f], loc.at[0])
    own_x = pltpu.make_async_copy(xs.at[me], xr.at[me], loc.at[1])
    own_vg = pltpu.make_async_copy(vg_ref.at[me], vgr.at[me], loc.at[2])
    own_mix = pltpu.make_async_copy(mixs.at[me], mixr.at[me], loc.at[3])
    for cp in (own_w, own_x, own_vg, own_mix):
        cp.start()

    def norm(i):
        total = jnp.zeros((TOK, 128), F32)
        for q in range(Q):
            part = x_ref[i, :, q * QW : (q + 1) * QW].astype(F32)
            part = part * part
            for b in range(QW // 128):
                total = total + part[:, b * 128 : (b + 1) * 128]
        inverse = lax.rsqrt(jnp.sum(total, axis=1, keepdims=True) / D + EPSILON)
        for q in range(Q):
            cols = slice(q * QW, (q + 1) * QW)
            nf[i, :, cols] = (x_ref[i, :, cols].astype(F32) * inverse * gain_ref[:, cols]).astype(BF16)

    each(0, 16, norm)

    def kept(d):
        chosen, _, _ = slot(d)
        for q in range(Q):
            a3[q, d] = nf[chosen, :, q * QW : (q + 1) * QW]

    each(0, 16, kept)
    ap_put = put(a3.at[pl.ds((1 - c) * 4, 4)], ap, ap_s.at[0], ap_s.at[1], partner)
    ap_put.start()

    own_vg.wait()
    each(1, 16, lambda k: put(vg_ref.at[0], vgr.at[(me + 16 - k) % 16], vg_s.at[k], vg_r.at[(me + 16 - k) % 16], partner).wait_recv())

    def add_bias(d, total):
        rows = vgr[d].astype(F32) * mixs[d][:, :1]
        vgr[d] = rows.astype(BF16)
        return total + rows

    bias_rows = lax.fori_loop(0, 16, add_bias, jnp.zeros((TOK, V), F32))
    vgp_put = put(vgr, vgp, vgp_s.at[0], vgp_s.at[1], partner)
    vgp_put.start()
    row = lax.broadcasted_iota(jnp.int32, (8, V), 0)
    mine = jnp.where(
        row == 0, jnp.sum(bias_rows, axis=0, keepdims=True),
        jnp.where(row == 1, kept_total, jnp.where(row == 2, kept_number, 0.0)),
    )
    st[0] = mine
    sty[y] = mine
    st_y = [put(st.at[0], sty.at[y], sty_s.at[k], sty_r.at[y], at(x, z, (y + k) % 4, c)) for k in (1, 2, 3)]
    for cp in st_y:
        cp.start()

    ap_put.wait_recv()
    vgp_put.wait_recv()

    def share(yq, store):
        for b in range(QW // 128):
            cols = slice(b * 128, (b + 1) * 128)
            both = (((0,), (0,)), ((), ()))
            left = a3[c * 4 + yq, :, :, cols].reshape(16 * TOK, 128)
            right = ap[yq, :, :, cols].reshape(16 * TOK, 128)
            part = lax.dot_general(left, vgr[...].reshape(16 * TOK, V), both, preferred_element_type=F32)
            part += lax.dot_general(right, vgp[...].reshape(16 * TOK, V), both, preferred_element_type=F32)
            store(cols, part)

    m_y = []
    for k in (2, 1, 3):
        yq = (y + k) % 4

        def to_send(cols, part, k=k):
            ms[k - 1, cols, :] = part.astype(BF16)

        share(yq, to_send)
        cp = put(ms.at[k - 1], mr.at[k - 1], my_s.at[k], my_r.at[k], at(x, z, yq, c))
        cp.start()
        m_y.append(cp)

    def to_own(cols, part):
        mown[cols, :] = part

    share(y, to_own)

    oz = (1 - zh) * 8 + c
    w_in = lambda slot_: put(w_ref, wf.at[slot_], w_s.at[0], w_r.at[slot_], partner)
    w_in(oz + y * 2).wait_recv()
    for k in (2, 1, 3):
        w_put(oz + y * 2, 5 + k + (k > 0), at(x, z, (y + k) % 4, c)).start()
    w_put(oz + y * 2, 10, partner).start()
    for k in (1, 3, 2):
        s = zh * 8 + ((y + k) % 4) * 2 + c
        w_in(s).wait_recv()
        w_put(s, 10 + k, partner).start()

    for k in (1, 2, 3):
        put(st.at[0], sty.at[(y + k) % 4], sty_s.at[k], sty_r.at[(y + k) % 4], partner).wait_recv()
    mine = ((sty[0] + sty[1]) + sty[2]) + sty[3]
    st[1] = mine
    stx[x] = mine
    st_x = [put(st.at[1], stx.at[x], stx_s.at[k], stx_r.at[x], at((x + k) % 4, z, y, c)) for k in (1, 2, 3)]
    for cp in st_x:
        cp.start()

    own_w.wait()
    acc[...] = jnp.zeros_like(acc)
    vg_all = vg_ref

    def block(q):
        rows = wf[pl.ds(q * 2, 2)].reshape(QW, V)
        acc[...] += jnp.dot(nf[:, :, lanes(q)].reshape(16 * TOK, QW), rows, preferred_element_type=F32)
        grad = lax.dot_general(
            vg_all[...].reshape(16 * TOK, V), rows, (((1,), (1,)), ((), ())), preferred_element_type=F32
        )
        ng[:, :, lanes(q)] = grad.reshape(16, TOK, QW)

    def first_blocks(k):
        yq = (y + k) % 4
        w_in(zh * 8 + yq * 2 + 1 - c).wait_recv()
        block(zh * 4 + yq)

    each(0, 4, first_blocks)
    w_in((1 - zh) * 8 + y * 2 + 1 - c).wait_recv()
    block((1 - zh) * 4 + y)

    for k in (1, 2, 3):
        put(st.at[0], stx.at[(x + k) % 4], stx_s.at[k], stx_r.at[(x + k) % 4], partner).wait_recv()
    mine = ((stx[0] + stx[1]) + stx[2]) + stx[3]
    st[2] = mine
    stz[z] = mine
    st_z = [put(st.at[2], stz.at[z], stz_s.at[k], stz_r.at[z], at(x, (z + k) % 8, y, c)) for k in range(1, 8)]
    for cp in st_z:
        cp.start()

    for k in (1, 2, 3):
        put(ms.at[0], mr.at[k - 1], my_s.at[k], my_r.at[k], partner).wait_recv()
    for b in range(QW // 128):
        cols = slice(b * 128, (b + 1) * 128)
        total = mown[cols, :] + mr[0, cols, :].astype(F32) + mr[1, cols, :].astype(F32) + mr[2, cols, :].astype(F32)
        mown[cols, :] = total
        mxs[cols, :] = total.astype(BF16)
    m_x = []
    for k in (2, 1, 3):
        xq = (x + k) % 4
        cp = put(
            mxs.at[pl.ds(pl.multiple_of(xq * 160, 32), 160)], mxr.at[k - 1], mx_s.at[k], mx_r.at[k], at(xq, z, y, c)
        )
        cp.start()
        m_x.append(cp)

    part = []
    for b in range(2):
        rows = mown[b * SH : (b + 1) * SH, :] * wf[(c * 4 + y) * 2 + b].astype(F32)
        part.append(rows[:, :128] + rows[:, 128:256] + rows[:, 256:384] + rows[:, 384:])
    gains = lax.dot_general(
        jnp.ones((8, 128), F32), jnp.concatenate(part, axis=0), (((1,), (1,)), ((), ())),
        precision=lax.Precision.HIGHEST, preferred_element_type=F32,
    )[:1]
    gs[0] = gains
    gx[x] = gains
    g_x = [put(gs.at[0], gx.at[x], gx_s.at[k], gx_r.at[x], at((x + k) % 4, z, y, c)) for k in (1, 2, 3)]
    for cp in g_x:
        cp.start()

    for k in (1, 2, 3):
        put(mxs.at[pl.ds(0, 160)], mxr.at[k - 1], mx_s.at[k], mx_r.at[k], partner).wait_recv()
    mx[...] = (
        mown[pl.ds(pl.multiple_of(x * 160, 32), 160), :]
        + mxr[0].astype(F32) + mxr[1].astype(F32) + mxr[2].astype(F32)
    )
    for b in range(4):
        mzs[b] = mx[b * 40 : (b + 1) * 40, :].astype(BF16)

    def z_put(k):
        zq = (z + k) % 8
        return put(mzs.at[zq % 4], mzr.at[z], mz_s.at[k], mz_r.at[z], at(x, zq, y, c))

    for k in range(1, 8):
        @pl.when((z + k) % 8 // 4 == c)
        def _(k=k):
            z_put(k).start()

    for k in (1, 2, 3):
        put(gs.at[0], gx.at[(x + k) % 4], gx_s.at[k], gx_r.at[(x + k) % 4], partner).wait_recv()
    gains = ((gx[0] + gx[1]) + gx[2]) + gx[3]
    gs[1] = gains
    gz[z] = gains
    g_z = [put(gs.at[1], gz.at[z], gz_s.at[k], gz_r.at[z], at(x, (z + k) % 8, y, c)) for k in range(1, 8)]
    for cp in g_z:
        cp.start()

    for k in (1, 3, 2):
        s = oz + ((y + k) % 4) * 2
        w_in(s).wait_recv()
        w_put(s, 13 + k, partner).start()

    def last_blocks(k):
        yq = (y + k) % 4
        w_in((1 - zh) * 8 + yq * 2 + 1 - c).wait_recv()
        block((1 - zh) * 4 + yq)

    each(1, 4, last_blocks)
    values_ref[...] = (acc[...] + bias_ref[...]).astype(BF16)

    for k in range(1, 8):
        zq = (z + k) % 8
        put(st.at[0], stz.at[zq], stz_s.at[k], stz_r.at[zq], partner).wait_recv()
    total = stz[0]
    for b in range(1, 8):
        total = total + stz[b]
    st[3] = total
    st_c = put(st.at[3], stc, stc_s.at[0], stc_s.at[1], partner)
    st_c.start()

    sums_here = zh == c
    to_core = x // 2
    place = (x % 2) * 4 + zl

    def ag_put(k):
        return put(ags, agr.at[place], ag_s.at[k], ag_r.at[place], ((me + k) % 16, zh * 8 + y * 2 + to_core))

    @pl.when(sums_here)
    def _():
        mzr[z] = mzs[zl]
        for k in range(1, 8):
            zq = (z + k) % 8
            put(mzs.at[0], mzr.at[zq], mz_s.at[k], mz_r.at[zq], partner).wait_recv()
        total = mzr[0].astype(F32)
        for b in range(1, 8):
            total += mzr[b].astype(F32)
        ags[...] = total.astype(BF16)
        each(1, 16, lambda k: ag_put(k).start())

        @pl.when(to_core == c)
        def _():
            agr[place] = ags[...]

        @pl.when(to_core != c)
        def _():
            ag_put(0).start()

    for k in range(1, 8):
        zq = (z + k) % 8
        put(gs.at[0], gz.at[zq], gz_s.at[k], gz_r.at[zq], partner).wait_recv()
    gains = gz[0]
    for b in range(1, 8):
        gains = gains + gz[b]
    gs[2] = gains
    mine_q = c * 4 + y
    gq[mine_q] = gains
    g_q = []
    for k in range(1, 8):
        cp = put(gs.at[2], gq.at[mine_q], gq_s.at[k], gq_r.at[mine_q], (me, zh * 8 + (f + k) % 8))
        cp.start()
        g_q.append(cp)

    st_c.wait_recv()
    total = st[3] + stc[...]
    ratio = total[2:3, 0:1] / total[1:2, 0:1]
    bgrad_ref[...] = total[0:1, :] * ratio

    own_x.wait()
    own_mix.wait()

    def slot_grad(s):
        squares = jnp.zeros((TOK, 128), F32)
        products = jnp.zeros((TOK, 128), F32)
        for q in range(Q):
            cols = slice(q * QW, (q + 1) * QW)
            rows = xr[s, :, cols].astype(F32)
            both = ng[s, :, cols] * gain_ref[:, cols] * rows
            rows = rows * rows
            for b in range(QW // 128):
                squares = squares + rows[:, b * 128 : (b + 1) * 128]
                products = products + both[:, b * 128 : (b + 1) * 128]
        inverse = lax.rsqrt(jnp.sum(squares, axis=1, keepdims=True) / D + EPSILON)
        mean = jnp.sum(products, axis=1, keepdims=True) / D
        scale = ratio * mixr[s][:, :1]
        left = inverse * scale
        right = inverse * inverse * inverse * mean * scale
        for q in range(Q):
            cols = slice(q * QW, (q + 1) * QW)
            rows = xr[s, :, cols].astype(F32)
            igrad_ref[s, :, cols] = (left * (ng[s, :, cols] * gain_ref[:, cols]) - rows * right).astype(BF16)

    slot_grad(me)

    def take(k):
        s = (me + 16 - k) % 16
        put(mixs.at[0], mixr.at[s], mix_s.at[k], mix_r.at[s], partner).wait_recv()
        put(xs.at[0], xr.at[s], x_s.at[k], x_r.at[s], partner).wait_recv()
        slot_grad(s)

    each(1, 16, take)

    for source in range(8):
        here = sums_here & (to_core == c) & (place == source)

        @pl.when(jnp.logical_not(here))
        def _(source=source):
            put(ags, agr.at[source], ag_s.at[0], ag_r.at[source], partner).wait_recv()

    for b in range(8):
        wgrad_ref[b * 40 : (b + 1) * 40, :] = agr[b].astype(F32) * ratio

    for k in range(1, 8):
        other = (f + k) % 8
        s = (other % 2) * 4 + other // 2
        put(gs.at[0], gq.at[s], gq_s.at[k], gq_r.at[s], partner).wait_recv()
    for q in range(Q):
        cols = slice(q * QW, (q + 1) * QW)
        ggrad_ref[:, cols] = gq[q] * ratio / gain_ref[:, cols]

    def sent(k):
        vg_put(k).wait_send()
        mix_put(k).wait_send()
        x_put(k).wait_send()

    each(1, 16, sent)

    @pl.when(edge)
    def _():
        w_put(f, 4, partner).wait_send()
        w_put(f, 5, partner).wait_send()

    for sem in (0, 1, 2, 3, 7, 8, 9, 10, 11, 12, 13, 14, 15, 16):
        w_put(f, sem, partner).wait_send()
    for cp in [ap_put, vgp_put, st_c] + st_y + st_x + st_z + m_y + m_x + g_x + g_z + g_q:
        cp.wait_send()
    for k in range(1, 8):
        @pl.when((z + k) % 8 // 4 == c)
        def _(k=k):
            z_put(k).wait_send()

    @pl.when(sums_here)
    def _():
        each(1, 16, lambda k: ag_put(k).wait_send())

        @pl.when(to_core != c)
        def _():
            ag_put(0).wait_send()


def body(
    layer_in, norm_gain, v_weight, v_bias, corpus, mixture, keep_count, keep_seq, keep_dest, value_grad
):
    vmem = pl.BlockSpec(memory_space=pltpu.VMEM)
    hbm = pl.BlockSpec(memory_space=pltpu.HBM)
    smem = pltpu.SMEM
    dma = pltpu.SemaphoreType.DMA
    values, input_grad, weight_grad, gain_grad, bias_grad = pl.pallas_call(
        kernel,
        out_shape=(
            pltpu.VMEM((16 * TOK, V), BF16),
            pltpu.VMEM((16, TOK, D), BF16),
            pltpu.VMEM((SH, V), F32),
            pltpu.VMEM((1, D), F32),
            pltpu.VMEM((1, V), F32),
        ),
        in_specs=[hbm] * 10,
        out_specs=[vmem] * 5,
        scratch_shapes=[
            pltpu.VMEM((16, TOK, D), BF16), pltpu.VMEM((1, D), F32), pltpu.VMEM((SH, V), BF16),
            pltpu.VMEM((1, V), F32), pltpu.VMEM((16, TOK, V), BF16),
            smem(corpus.shape, jnp.int32), smem(mixture.shape, jnp.int32), smem((1,), jnp.int32),
            smem(keep_seq.shape[2:], jnp.int32), smem(keep_dest.shape[2:], jnp.int32),
            pltpu.VMEM((16, TOK, D), BF16),
            pltpu.VMEM((16, TOK, D), BF16),
            pltpu.VMEM((16, 1, 128), F32),
            pltpu.VMEM((16, 1, 128), F32),
            pltpu.VMEM((16, TOK, D), BF16),
            pltpu.VMEM((Q, 16, TOK, QW), BF16),
            pltpu.VMEM((4, 16, TOK, QW), BF16),
            pltpu.VMEM((16, TOK, V), BF16),
            pltpu.VMEM((16, TOK, V), BF16),
            pltpu.VMEM((NF, SH, V), BF16),
            pltpu.VMEM((16 * TOK, V), F32),
            pltpu.VMEM((16, TOK, D), F32),
            pltpu.VMEM((3, QW, V), BF16),
            pltpu.VMEM((3, QW, V), BF16),
            pltpu.VMEM((QW, V), F32),
            pltpu.VMEM((QW, V), BF16),
            pltpu.VMEM((3, QW // 4, V), BF16),
            pltpu.VMEM((QW // 4, V), F32),
            pltpu.VMEM((4, QW // 16, V), BF16),
            pltpu.VMEM((8, QW // 16, V), BF16),
            pltpu.VMEM((QW // 16, V), BF16),
            pltpu.VMEM((8, QW // 16, V), BF16),
            pltpu.VMEM((3, 1, QW), F32),
            pltpu.VMEM((4, 1, QW), F32),
            pltpu.VMEM((8, 1, QW), F32),
            pltpu.VMEM((Q, 1, QW), F32),
            pltpu.VMEM((4, 8, V), F32),
            pltpu.VMEM((4, 8, V), F32),
            pltpu.VMEM((4, 8, V), F32),
            pltpu.VMEM((8, 8, V), F32),
            pltpu.VMEM((8, V), F32),
            dma((16,)), dma((16,)), dma((16,)), dma((16,)), dma((16,)), dma((16,)),
            dma((17,)), dma((16,)), dma((2,)), dma((2,)),
            dma((4,)), dma((4,)), dma((4,)), dma((4,)), dma((8,)), dma((8,)),
            dma((16,)), dma((8,)),
            dma((4,)), dma((4,)), dma((8,)), dma((8,)), dma((8,)), dma((8,)),
            dma((4,)), dma((4,)), dma((4,)), dma((4,)), dma((8,)), dma((8,)), dma((2,)), dma((14,)),
        ],
        compiler_params=pltpu.CompilerParams(
            collective_id=0, has_side_effects=True, vmem_limit_bytes=57 * 1024 * 1024
        ),
        name="step",
    )(
        layer_in, norm_gain[None, :], v_weight, v_bias[None, :], value_grad[0, 0],
        corpus, mixture, keep_count[0], keep_seq[0, 0], keep_dest[0, 0],
    )
    return (
        values.reshape(16, TOK, V), input_grad[None, None], weight_grad, gain_grad[0], bias_grad[0],
    )


def solution(mesh):
    return jax.shard_map(
        body,
        mesh=mesh,
        in_specs=(
            P(("dp", "fsdp"), None, None),
            P(),
            P("fsdp", None),
            P(),
            P(("dp", "fsdp")),
            P(),
            P("dp", "fsdp"),
            P("dp", "fsdp", None),
            P("dp", "fsdp", None),
            P("dp", "fsdp", None, None, None),
        ),
        out_specs=(
            P(("dp", "fsdp"), None, None),
            P("dp", "fsdp", None, None, None),
            P("fsdp", None),
            P(),
            P(),
        ),
        check_vma=False,
    )
```

```python
import jax
import jax.numpy as jnp
from jax import lax
from jax.experimental import pallas as pl
from jax.experimental.pallas import tpu as pltpu
from jax.sharding import PartitionSpec as P

EPSILON = 1e-06
MESH = pl.DeviceIdType.MESH
F32 = jnp.float32
BF16 = jnp.bfloat16

NX, NZ, NY, NC = 4, 4, 4, 2
NDP, NF = 16, 16
TOK = 16
D, V = 5120, 512
Q = 8
QW = D // Q
SH = D // NF


def put(src, dst, send, recv, device):
    return pltpu.make_async_remote_copy(
        src_ref=src, dst_ref=dst, send_sem=send, recv_sem=recv, device_id=device, device_id_type=MESH
    )


def lanes(q):
    return pl.ds(pl.multiple_of(q * QW, 128), QW)


def kernel(
    x_hbm, gain_hbm, w_hbm, bias_hbm, vg_hbm, corpus_hbm, mixture_hbm, count_hbm, seq_hbm, dest_hbm,
    values_out, igrad_out, wgrad_out, ggrad_ref, bgrad_ref,
    values_ref, igrad_ref, wgrad_ref,
    x_ref, gain_ref, w_ref, bias_ref, vg_ref, corpus_ref, mixture_ref, count_ref, seq_ref, dest_ref,
    xs, xr, mixs, mixr, nf, a3, ap, vgr, vgp, wf, acc, ng,
    msf, mp, msd, msc, mrf, mrd, mrc, mown, mxs, mxr, mx, mzs, mzr, ags, agr, gs, gx, gz, gq, st, sty, stx, stz, stc,
    vg_s, vg_r, x_s, x_r, mix_s, mix_r, w_s, w_r, w_r2, ap_s, vgp_s, my_s, my_r, mx_s, mx_r, mz_s, mz_r,
    az_s, az_r, ag_s, ag_r, gx_s, gx_r, gz_s, gz_r, gq_s, gq_r, sty_s, sty_r, stx_s, stx_r, stz_s, stz_r, stc_s, loc, ig_s,
):
    me = lax.axis_index("dp")
    f = lax.axis_index("fsdp")
    x, zl = me // NZ, me % NZ
    zh, y, c = f // 8, (f // 2) % NY, f % 2
    z = zh * 4 + zl

    def at(x_, z_, y_, c_):
        return (x_ * NZ + z_ % 4, (z_ // 4) * 8 + y_ * 2 + c_)

    partner = (me, zh * 8 + y * 2 + 1 - c)

    moves = [
        pltpu.make_async_copy(src, dst, loc.at[4 + i])
        for i, (src, dst) in enumerate((
            (corpus_hbm, corpus_ref), (mixture_hbm, mixture_ref), (count_hbm, count_ref), (seq_hbm, seq_ref),
            (dest_hbm, dest_ref), (x_hbm, x_ref), (vg_hbm, vg_ref), (w_hbm, w_ref), (gain_hbm, gain_ref),
            (bias_hbm, bias_ref),
        ))
    ]
    for cp in moves:
        cp.start()

    bar = pltpu.get_barrier_semaphore()
    greeted = 0
    for k in range(1, 16):
        other = (me + k) % 16
        for dev in ((other, f), (other, partner[1])):
            pl.semaphore_signal(bar, inc=1, device_id=dev, device_id_type=MESH)
            greeted += 1
    for k in range(1, 8):
        pl.semaphore_signal(bar, inc=1, device_id=(me, zh * 8 + (f + k) % 8), device_id_type=MESH)
        greeted += 1
    for k in range(4):
        pl.semaphore_signal(
            bar, inc=1, device_id=(x * NZ + k, (1 - zh) * 8 + y * 2 + c), device_id_type=MESH
        )
        greeted += 1
    for cp in moves[:6]:
        cp.wait()

    def slot(d):
        chosen, live = jnp.int32(0), jnp.int32(0)
        for j in range(dest_ref.shape[0]):
            hit = (dest_ref[j] == d) & (j < count_ref[0])
            chosen = jnp.where(hit, seq_ref[j], chosen)
            live = jnp.where(hit, 1, live)
        mix = mixture_ref[corpus_ref[chosen]] * live
        return chosen, live, mix.astype(F32)

    def gather(d, carry):
        total, number = carry
        chosen, live, mix = slot(d)
        xs[d] = x_ref[chosen]
        mixs[d] = jnp.broadcast_to(mix, (1, 128))
        return total + mix, number + live.astype(F32)

    kept_total, kept_number = lax.fori_loop(0, 16, gather, (jnp.float32(0), jnp.float32(0)))

    for cp in moves[6:]:
        cp.wait()
    pl.semaphore_wait(bar, greeted)

    def vg_put(k):
        d = (me + k) % 16
        return put(vg_ref.at[d], vgr.at[me], vg_s.at[0], vg_r.at[0], (d, f))

    def mix_put(k):
        d = (me + k) % 16
        return put(mixs.at[d], mixr.at[me], mix_s.at[0], mix_r.at[0], (d, f))

    def other_dp(dx, m):
        z_ = zl + m - 2 * ((zl % 2) * (m % 2) + (zl // 2) * (m // 2) * 2)
        return (x + dx) % 4 * NZ + z_

    def x_put(dx, m):
        d = other_dp(dx, m)
        return put(xs.at[d], xr.at[me], x_s.at[0], x_r.at[me], (d, f))

    def w_put(slot_, sem, dev, own=False):
        return put(w_ref if own else wf.at[slot_], wf.at[slot_], w_s.at[sem], w_r.at[slot_], dev)

    def w_half(slot_, half, sem, dev):
        rows = wf.at[slot_, pl.ds(half * (SH // 2), SH // 2)]
        return put(rows, rows, w_s.at[sem], (w_r2 if half else w_r).at[slot_], dev)

    def each(start, stop, fn):
        def step(i, carry):
            fn(i)
            return carry

        lax.fori_loop(start, stop, step, 0)

    y_up, y_down = at(x, z, (y + 1) % 4, c), at(x, z, (y + 3) % 4, c)
    each(1, 16, lambda k: vg_put(k).start())
    edge = (zl == 0) | (zl == 3)
    far = (1 - zh) * 4 + jnp.where(zl == 0, 3, 0)
    near = (1 - zh) * 4 + jnp.where(zl == 0, 2, 1)

    @pl.when(edge)
    def _():
        w_put(f, 1, at(x, far, y, c), True).start()
        w_put(f, 1, at(x, near, y, c), True).start()

    w_put(f, 0, y_up, True).start()
    w_put(f, 0, y_down, True).start()
    w_put(f, 0, partner, True).start()
    each(1, 16, lambda k: mix_put(k).start())

    across = tuple(((1 + i // 2) % 4, 2 + i % 2) for i in range(8))
    beside = ((1, 1), (2, 1), (3, 1), (0, 1))
    along_x = ((1, 0), (3, 0), (2, 0))

    def x_go(pairs):
        for dx, m in pairs:
            x_put(dx, m).start()

    own_w = pltpu.make_async_copy(w_ref, wf.at[f], loc.at[0])
    own_x = pltpu.make_async_copy(xs.at[me], xr.at[me], loc.at[1])
    own_vg = pltpu.make_async_copy(vg_ref.at[me], vgr.at[me], loc.at[2])
    own_mix = pltpu.make_async_copy(mixs.at[me], mixr.at[me], loc.at[3])
    for cp in (own_w, own_x, own_vg, own_mix):
        cp.start()

    x_go(across[:5] + beside[:1] + along_x)
    def norm(i):
        total = jnp.zeros((TOK, 128), F32)
        for q in range(Q):
            part = x_ref[i, :, q * QW : (q + 1) * QW].astype(F32)
            part = part * part
            for b in range(QW // 128):
                total = total + part[:, b * 128 : (b + 1) * 128]
        inverse = lax.rsqrt(jnp.sum(total, axis=1, keepdims=True) / D + EPSILON)
        for q in range(Q):
            cols = slice(q * QW, (q + 1) * QW)
            nf[i, :, cols] = (x_ref[i, :, cols].astype(F32) * inverse * gain_ref[:, cols]).astype(BF16)

    each(0, 16, norm)

    def kept(d):
        chosen, _, _ = slot(d)
        for q in range(Q):
            a3[q, d] = nf[chosen, :, q * QW : (q + 1) * QW]

    each(0, 16, kept)
    ap_put = put(a3.at[pl.ds((1 - c) * 4, 4)], ap, ap_s.at[0], ap_s.at[1], partner)
    ap_put.start()

    own_vg.wait()
    all_vg = put(vg_ref.at[pl.ds(0, 15)], vgr.at[pl.ds(0, 15)], vg_s.at[0], vg_r.at[0], partner)
    all_vg.wait_recv()
    all_mix = put(mixs.at[pl.ds(0, 15)], mixr.at[pl.ds(0, 15)], mix_s.at[0], mix_r.at[0], partner)

    sa, sb, sf = (zh * 8 + ((y + k) % 4) * 2 + c for k in (1, 3, 2))
    w_in = lambda slot_: put(w_ref, wf.at[slot_], w_s.at[0], w_r.at[slot_], partner)
    w_in(sb).wait_recv()
    w_half(sb, 0, 0, y_up).start()
    w_in(sa).wait_recv()
    w_half(sa, 1, 0, y_down).start()
    w_put(sa, 0, partner).start()
    w_put(sb, 0, partner).start()

    def add_bias(d, total):
        rows = vgr[d].astype(F32) * mixs[d][:, :1]
        vgr[d] = rows.astype(BF16)
        return total + rows

    bias_rows = lax.fori_loop(0, 16, add_bias, jnp.zeros((TOK, V), F32))
    vgp_put = put(vgr, vgp, vgp_s.at[0], vgp_s.at[1], partner)
    vgp_put.start()
    lane = lax.broadcasted_iota(jnp.int32, (1, 128), 1)
    tail = jnp.where(lane == 0, kept_total, jnp.where(lane == 1, kept_number, 0.0))
    mine = jnp.concatenate([jnp.sum(bias_rows, axis=0, keepdims=True), tail], axis=1)
    st[0] = mine
    sty[y] = mine
    st_y = [put(st.at[0], sty.at[y], sty_s.at[0], sty_r.at[0], at(x, z, (y + k) % 4, c)) for k in (1, 2, 3)]
    for cp in st_y:
        cp.start()

    ap_put.wait_recv()
    vgp_put.wait_recv()

    def share(yq, store):
        for b in range(QW // 128):
            cols = slice(b * 128, (b + 1) * 128)
            both = (((0,), (0,)), ((), ()))
            left = a3[c * 4 + yq, :, :, cols].reshape(16 * TOK, 128)
            right = ap[yq, :, :, cols].reshape(16 * TOK, 128)
            part = lax.dot_general(left, vgr[...].reshape(16 * TOK, V), both, preferred_element_type=F32)
            part += lax.dot_general(right, vgp[...].reshape(16 * TOK, V), both, preferred_element_type=F32)
            store(cols, part)

    def to_far(cols, part):
        msf[cols, :] = part.astype(BF16)

    def m_put(kind, way, src, dst):
        return put(src, dst, my_s.at[0], my_r.at[kind * 2 + way], y_down if way else y_up)

    half = SH
    m_far = lambda way: m_put(0, way, msf.at[pl.ds(way * half, half)], mrf.at[way])
    m_near = lambda way: m_put(1, way, msd.at[way], mrd.at[way])
    m_both = lambda way: m_put(2, way, msc.at[way], mrc.at[way])
    share((y + 2) % 4, to_far)
    for way in (0, 1):
        m_far(way).start()
    for way, k in ((0, 1), (1, 3)):
        def to_part(cols, part, way=way):
            mp[way, cols, :] = part

        share((y + k) % 4, to_part)
        msd[way] = mp[way, (1 - way) * half : (2 - way) * half, :].astype(BF16)
        m_near(way).start()

    def to_own(cols, part):
        mown[cols, :] = part

    share(y, to_own)

    for h in (0, 1):
        w_half(sf, h, 0, partner).wait_recv()
    w_put(sf, 0, partner).start()

    all_y = put(sty.at[pl.ds(0, 3)], sty.at[pl.ds(0, 3)], sty_s.at[0], sty_r.at[0], partner)
    all_y.wait_recv()
    mine = ((sty[0] + sty[1]) + sty[2]) + sty[3]
    st[1] = mine
    stx[x] = mine
    st_x = [put(st.at[1], stx.at[x], stx_s.at[0], stx_r.at[0], at((x + k) % 4, z, y, c)) for k in (1, 2, 3)]
    for cp in st_x:
        cp.start()

    own_w.wait()
    acc[...] = jnp.zeros_like(acc)
    vg_all = vg_ref

    def block(q):
        rows = wf[pl.ds(q * 2, 2)].reshape(QW, V)
        acc[...] += jnp.dot(nf[:, :, lanes(q)].reshape(16 * TOK, QW), rows, preferred_element_type=F32)
        grad = lax.dot_general(
            vg_all[...].reshape(16 * TOK, V), rows, (((1,), (1,)), ((), ())), preferred_element_type=F32
        )
        ng[:, :, lanes(q)] = grad.reshape(16, TOK, QW)

    def first_blocks(k):
        yq = (y + k) % 4
        w_in(zh * 8 + yq * 2 + 1 - c).wait_recv()
        block(zh * 4 + yq)

    each(0, 4, first_blocks)

    for way in (0, 1):
        m_far(way).wait_recv()
        msc[way] = (mp[way, way * half : (way + 1) * half, :] + mrf[way].astype(F32)).astype(BF16)
        m_both(way).start()

    oz = (1 - zh) * 8 + c
    w_in(oz + y * 2).wait_recv()
    w_put(oz + y * 2, 0, y_up).start()
    w_put(oz + y * 2, 0, y_down).start()
    w_put(oz + y * 2, 0, partner).start()
    w_in((1 - zh) * 8 + y * 2 + 1 - c).wait_recv()
    block((1 - zh) * 4 + y)

    all_x = put(stx.at[pl.ds(0, 3)], stx.at[pl.ds(0, 3)], stx_s.at[0], stx_r.at[0], partner)
    all_x.wait_recv()
    mine = ((stx[0] + stx[1]) + stx[2]) + stx[3]
    st[2] = mine
    stz[z] = mine
    st_z = [put(st.at[2], stz.at[z], stz_s.at[0], stz_r.at[0], at(x, (z + k) % 8, y, c)) for k in range(1, 8)]
    for cp in st_z:
        cp.start()

    x_go(across[5:6] + beside[1:2])

    for way in (0, 1):
        m_near(way).wait_recv()
        m_both(way).wait_recv()
    for way in (0, 1):
        rows = slice(way * half, (way + 1) * half)
        total = mown[rows, :] + mrc[way].astype(F32) + mrd[1 - way].astype(F32)
        mown[rows, :] = total
        mxs[rows, :] = total.astype(BF16)
    m_x = []
    for k in (2, 1, 3):
        xq = (x + k) % 4
        cp = put(
            mxs.at[pl.ds(pl.multiple_of(xq * 160, 32), 160)], mxr.at[k - 1], mx_s.at[0], mx_r.at[0], at(xq, z, y, c)
        )
        cp.start()
        m_x.append(cp)

    x_go(across[6:7])

    ta, tb, tf = (oz + ((y + k) % 4) * 2 for k in (1, 3, 2))
    w_in(tb).wait_recv()
    w_half(tb, 0, 0, y_up).start()
    w_in(ta).wait_recv()
    w_half(ta, 1, 0, y_down).start()
    w_put(ta, 0, partner).start()
    w_put(tb, 0, partner).start()

    part = []
    for b in range(2):
        rows = mown[b * SH : (b + 1) * SH, :] * wf[(c * 4 + y) * 2 + b].astype(F32)
        part.append(rows[:, :128] + rows[:, 128:256] + rows[:, 256:384] + rows[:, 384:])
    gains = lax.dot_general(
        jnp.ones((8, 128), F32), jnp.concatenate(part, axis=0), (((1,), (1,)), ((), ())),
        precision=lax.Precision.HIGHEST, preferred_element_type=F32,
    )[:1]
    gs[0] = gains
    gx[x] = gains
    g_x = [put(gs.at[0], gx.at[x], gx_s.at[0], gx_r.at[0], at((x + k) % 4, z, y, c)) for k in (1, 2, 3)]
    for cp in g_x:
        cp.start()

    all_mx = put(mxr, mxr, mx_s.at[0], mx_r.at[0], partner)
    all_mx.wait_recv()
    mx[...] = (
        mown[pl.ds(pl.multiple_of(x * 160, 32), 160), :]
        + mxr[0].astype(F32) + mxr[1].astype(F32) + mxr[2].astype(F32)
    )
    for b in range(4):
        mzs[b] = mx[b * 40 : (b + 1) * 40, :].astype(BF16)

    def z_put(k):
        zq = (z + k) % 8
        return put(mzs.at[zq % 4], mzr.at[z], mz_s.at[0], mz_r.at[0], at(x, zq, y, c))

    for k in range(1, 8):
        @pl.when((z + k) % 8 // 4 == c)
        def _(k=k):
            z_put(k).start()

    all_gx = put(gx.at[pl.ds(0, 3)], gx.at[pl.ds(0, 3)], gx_s.at[0], gx_r.at[0], partner)
    all_gx.wait_recv()
    gains = ((gx[0] + gx[1]) + gx[2]) + gx[3]
    gs[1] = gains
    gz[z] = gains
    g_z = [put(gs.at[1], gz.at[z], gz_s.at[0], gz_r.at[0], at(x, (z + k) % 8, y, c)) for k in range(1, 8)]
    for cp in g_z:
        cp.start()

    x_go(across[7:])

    for h in (0, 1):
        w_half(tf, h, 0, partner).wait_recv()
    w_put(tf, 0, partner).start()

    def last_blocks(k):
        yq = (y + k + k // 2 + 2 * (k // 3)) % 4
        w_in((1 - zh) * 8 + yq * 2 + 1 - c).wait_recv()
        block((1 - zh) * 4 + yq)

    each(1, 4, last_blocks)
    values_ref[...] = (acc[...] + bias_ref[...]).astype(BF16)
    values_copy = pltpu.make_async_copy(values_ref, values_out, loc.at[14])
    values_copy.start()

    all_z = put(stz.at[pl.ds(0, 7)], stz.at[pl.ds(0, 7)], stz_s.at[0], stz_r.at[0], partner)
    all_z.wait_recv()
    total = stz[0]
    for b in range(1, 8):
        total = total + stz[b]
    st[3] = total
    st_c = put(st.at[3], stc, stc_s.at[0], stc_s.at[1], partner)
    st_c.start()

    sums_here = zh == c
    to_core = x // 2

    def az_put(k):
        return put(ags.at[zl], ags.at[zl], az_s.at[0], az_r.at[0], at(x, zh * 4 + (zl + k) % 4, y, c))

    @pl.when(sums_here)
    def _():
        mzr[z] = mzs[zl]
        put(mzr.at[pl.ds(0, 7)], mzr.at[pl.ds(0, 7)], mz_s.at[0], mz_r.at[0], partner).wait_recv()
        total = mzr[0].astype(F32)
        for b in range(1, 8):
            total += mzr[b].astype(F32)
        ags[zl] = total.astype(BF16)
        for k in (2, 1, 3):
            az_put(k).start()

    x_go(beside[2:])

    all_gz = put(gz.at[pl.ds(0, 7)], gz.at[pl.ds(0, 7)], gz_s.at[0], gz_r.at[0], partner)
    all_gz.wait_recv()
    gains = gz[0]
    for b in range(1, 8):
        gains = gains + gz[b]
    gs[2] = gains
    mine_q = c * 4 + y
    gq[mine_q] = gains
    g_q = []
    for k in range(1, 8):
        cp = put(gs.at[2], gq.at[mine_q], gq_s.at[0], gq_r.at[0], (me, zh * 8 + (f + k) % 8))
        cp.start()
        g_q.append(cp)

    st_c.wait_recv()
    total = st[3] + stc[...]
    ratio = total[:, V + 1 : V + 2] / total[:, V : V + 1]
    bgrad_ref[...] = total[:, :V] * ratio

    own_x.wait()
    own_mix.wait()
    all_mix.wait_recv()

    def slot_copy(s):
        return pltpu.make_async_copy(igrad_ref.at[s], igrad_out.at[s], ig_s.at[0])

    def slot_grad(s):
        squares = jnp.zeros((TOK, 128), F32)
        products = jnp.zeros((TOK, 128), F32)
        for q in range(Q):
            cols = slice(q * QW, (q + 1) * QW)
            rows = xr[s, :, cols].astype(F32)
            both = ng[s, :, cols] * gain_ref[:, cols] * rows
            rows = rows * rows
            for b in range(QW // 128):
                squares = squares + rows[:, b * 128 : (b + 1) * 128]
                products = products + both[:, b * 128 : (b + 1) * 128]
        inverse = lax.rsqrt(jnp.sum(squares, axis=1, keepdims=True) / D + EPSILON)
        mean = jnp.sum(products, axis=1, keepdims=True) / D
        scale = ratio * mixr[s][:, :1]
        left = inverse * scale
        right = inverse * inverse * inverse * mean * scale
        for q in range(Q):
            cols = slice(q * QW, (q + 1) * QW)
            rows = xr[s, :, cols].astype(F32)
            igrad_ref[s, :, cols] = (left * (ng[s, :, cols] * gain_ref[:, cols]) - rows * right).astype(BF16)
        slot_copy(s).start()

    slot_grad(me)

    def take(dx, m):
        s = other_dp(4 - dx, m)
        put(xs.at[0], xr.at[s], x_s.at[0], x_r.at[s], partner).wait_recv()
        slot_grad(s)

    each(1, 4, lambda i: take(i, 0))
    each(0, 5, lambda i: take((1 + i // 2) % 4, 2 + i % 2))

    @pl.when(sums_here)
    def _():
        put(mzr.at[pl.ds(0, 3)], ags.at[pl.ds(0, 3)], az_s.at[0], az_r.at[0], partner).wait_recv()
        for k in (2, 1, 3):
            put(ags, agr.at[x % 2], ag_s.at[k - 1], ag_r.at[x % 2], at((x + k) % 4, z, y, to_core)).start()

        @pl.when(to_core == c)
        def _():
            agr[x % 2] = ags[...]

        @pl.when(to_core != c)
        def _():
            put(ags, agr.at[x % 2], ag_s.at[3], ag_r.at[x % 2], partner).start()

    each(5, 8, lambda i: take((1 + i // 2) % 4, 2 + i % 2))
    each(1, 5, lambda i: take(i % 4, 1))

    for b in range(2):
        here = sums_here & (to_core == c) & (x % 2 == b)

        @pl.when(jnp.logical_not(here))
        def _(b=b):
            put(agr.at[b], agr.at[b], ag_s.at[0], ag_r.at[b], partner).wait_recv()

    for b in range(2):
        for k in range(4):
            wgrad_ref[(b * 4 + k) * 40 : (b * 4 + k + 1) * 40, :] = agr[b, k].astype(F32) * ratio
    wgrad_copy = pltpu.make_async_copy(wgrad_ref, wgrad_out, loc.at[15])
    wgrad_copy.start()

    all_gq = put(gq.at[pl.ds(0, 7)], gq.at[pl.ds(0, 7)], gq_s.at[0], gq_r.at[0], partner)
    all_gq.wait_recv()
    for q in range(Q):
        cols = slice(q * QW, (q + 1) * QW)
        ggrad_ref[:, cols] = gq[q] * ratio / gain_ref[:, cols]

    values_copy.wait()
    wgrad_copy.wait()
    pltpu.make_async_copy(igrad_ref, igrad_out, ig_s.at[0]).wait()
    all_vg.wait_send()
    all_mix.wait_send()
    put(xs.at[pl.ds(0, 15)], xr.at[pl.ds(0, 15)], x_s.at[0], x_r.at[0], partner).wait_send()

    @pl.when(edge)
    def _():
        put(wf.at[pl.ds(0, 2)], wf.at[pl.ds(0, 2)], w_s.at[1], w_r.at[0], partner).wait_send()

    put(wf.at[pl.ds(0, 14)], wf.at[pl.ds(0, 14)], w_s.at[0], w_r.at[0], partner).wait_send()
    put(wf.at[pl.ds(0, 6)], wf.at[pl.ds(0, 6)], my_s.at[0], w_r.at[0], partner).wait_send()
    for cp in (ap_put, vgp_put, st_c, all_y, all_x, all_z, all_gx, all_gz, all_gq, all_mx):
        cp.wait_send()
    @pl.when(sums_here)
    def _():
        put(mzs.at[pl.ds(0, 3)], mzr.at[pl.ds(0, 3)], mz_s.at[0], mz_r.at[0], partner).wait_send()
        put(mzr.at[pl.ds(0, 3)], mzr.at[pl.ds(0, 3)], az_s.at[0], az_r.at[0], partner).wait_send()
        put(agr.at[0], agr.at[0], ag_s.at[0], ag_r.at[0], partner).wait_send()
        put(agr.at[0], agr.at[0], ag_s.at[1], ag_r.at[0], partner).wait_send()
        put(agr.at[0], agr.at[0], ag_s.at[2], ag_r.at[0], partner).wait_send()

        @pl.when(to_core != c)
        def _():
            put(agr.at[0], agr.at[0], ag_s.at[3], ag_r.at[0], partner).wait_send()

    @pl.when(jnp.logical_not(sums_here))
    def _():
        put(mzs, mzs, mz_s.at[0], mz_r.at[0], partner).wait_send()


def body(
    layer_in, norm_gain, v_weight, v_bias, corpus, mixture, keep_count, keep_seq, keep_dest, value_grad
):
    vmem = pl.BlockSpec(memory_space=pltpu.VMEM)
    hbm = pl.BlockSpec(memory_space=pltpu.HBM)
    smem = pltpu.SMEM
    dma = pltpu.SemaphoreType.DMA
    values, input_grad, weight_grad, gain_grad, bias_grad = pl.pallas_call(
        kernel,
        out_shape=(
            pltpu.VMEM((16 * TOK, V), BF16),
            pltpu.VMEM((16, TOK, D), BF16),
            pltpu.VMEM((SH, V), F32),
            pltpu.VMEM((1, D), F32),
            pltpu.VMEM((1, V), F32),
        ),
        in_specs=[hbm] * 10,
        out_specs=[pl.BlockSpec(memory_space=pl.ANY)] * 3 + [vmem] * 2,
        scratch_shapes=[
            pltpu.VMEM((16 * TOK, V), BF16), pltpu.VMEM((16, TOK, D), BF16), pltpu.VMEM((SH, V), F32),
            pltpu.VMEM((16, TOK, D), BF16), pltpu.VMEM((1, D), F32), pltpu.VMEM((SH, V), BF16),
            pltpu.VMEM((1, V), F32), pltpu.VMEM((16, TOK, V), BF16),
            smem(corpus.shape, jnp.int32), smem(mixture.shape, jnp.int32), smem((1,), jnp.int32),
            smem(keep_seq.shape[2:], jnp.int32), smem(keep_dest.shape[2:], jnp.int32),
            pltpu.VMEM((16, TOK, D), BF16),
            pltpu.VMEM((16, TOK, D), BF16),
            pltpu.VMEM((16, 1, 128), F32),
            pltpu.VMEM((16, 1, 128), F32),
            pltpu.VMEM((16, TOK, D), BF16),
            pltpu.VMEM((Q, 16, TOK, QW), BF16),
            pltpu.VMEM((4, 16, TOK, QW), BF16),
            pltpu.VMEM((16, TOK, V), BF16),
            pltpu.VMEM((16, TOK, V), BF16),
            pltpu.VMEM((NF, SH, V), BF16),
            pltpu.VMEM((16 * TOK, V), F32),
            pltpu.VMEM((16, TOK, D), F32),
            pltpu.VMEM((QW, V), BF16),
            pltpu.VMEM((2, QW, V), F32),
            pltpu.VMEM((2, SH, V), BF16),
            pltpu.VMEM((2, SH, V), BF16),
            pltpu.VMEM((2, SH, V), BF16),
            pltpu.VMEM((2, SH, V), BF16),
            pltpu.VMEM((2, SH, V), BF16),
            pltpu.VMEM((QW, V), F32),
            pltpu.VMEM((QW, V), BF16),
            pltpu.VMEM((3, QW // 4, V), BF16),
            pltpu.VMEM((QW // 4, V), F32),
            pltpu.VMEM((4, QW // 16, V), BF16),
            pltpu.VMEM((8, QW // 16, V), BF16),
            pltpu.VMEM((4, QW // 16, V), BF16),
            pltpu.VMEM((2, 4, QW // 16, V), BF16),
            pltpu.VMEM((3, 1, QW), F32),
            pltpu.VMEM((4, 1, QW), F32),
            pltpu.VMEM((8, 1, QW), F32),
            pltpu.VMEM((Q, 1, QW), F32),
            pltpu.VMEM((4, 1, V + 128), F32),
            pltpu.VMEM((4, 1, V + 128), F32),
            pltpu.VMEM((4, 1, V + 128), F32),
            pltpu.VMEM((8, 1, V + 128), F32),
            pltpu.VMEM((1, V + 128), F32),
            dma((1,)), dma((1,)), dma((1,)), dma((16,)), dma((1,)), dma((1,)),
            dma((2,)), dma((16,)), dma((16,)), dma((2,)), dma((2,)),
            dma((1,)), dma((6,)), dma((1,)), dma((1,)), dma((1,)), dma((1,)),
            dma((1,)), dma((1,)), dma((4,)), dma((2,)),
            dma((1,)), dma((1,)), dma((1,)), dma((1,)), dma((1,)), dma((1,)),
            dma((1,)), dma((1,)), dma((1,)), dma((1,)), dma((1,)), dma((1,)), dma((2,)), dma((16,)), dma((1,)),
        ],
        compiler_params=pltpu.CompilerParams(
            collective_id=0, has_side_effects=True, vmem_limit_bytes=57 * 1024 * 1024
        ),
        name="step",
    )(
        layer_in, norm_gain[None, :], v_weight, v_bias[None, :], value_grad[0, 0],
        corpus, mixture, keep_count[0], keep_seq[0, 0], keep_dest[0, 0],
    )
    return (
        values.reshape(16, TOK, V), input_grad[None, None], weight_grad, gain_grad[0], bias_grad[0],
    )


def solution(mesh):
    return jax.shard_map(
        body,
        mesh=mesh,
        in_specs=(
            P(("dp", "fsdp"), None, None),
            P(),
            P("fsdp", None),
            P(),
            P(("dp", "fsdp")),
            P(),
            P("dp", "fsdp"),
            P("dp", "fsdp", None),
            P("dp", "fsdp", None),
            P("dp", "fsdp", None, None, None),
        ),
        out_specs=(
            P(("dp", "fsdp"), None, None),
            P("dp", "fsdp", None, None, None),
            P("fsdp", None),
            P(),
            P(),
        ),
        check_vma=False,
    )
```

```python
import jax
import jax.numpy as jnp
from jax import lax
from jax.experimental import pallas as pl
from jax.experimental.pallas import tpu as pltpu
from jax.sharding import PartitionSpec as P

EPSILON = 1e-06
MESH = pl.DeviceIdType.MESH
F32 = jnp.float32
BF16 = jnp.bfloat16

NX, NZ, NY, NC = 4, 4, 4, 2
NDP, NF = 16, 16
TOK = 16
D, V = 5120, 512
Q = 8
QW = D // Q
SH = D // NF


def put(src, dst, send, recv, device):
    return pltpu.make_async_remote_copy(
        src_ref=src, dst_ref=dst, send_sem=send, recv_sem=recv, device_id=device, device_id_type=MESH
    )


def lanes(q):
    return pl.ds(pl.multiple_of(q * QW, 128), QW)


def kernel(
    x_hbm, gain_hbm, w_hbm, bias_hbm, vg_hbm, corpus_hbm, mixture_hbm, count_hbm, seq_hbm, dest_hbm,
    values_out, igrad_out, wgrad_out, ggrad_ref, bgrad_ref,
    values_ref, igrad_ref, wgrad_ref,
    x_ref, gain_ref, w_ref, bias_ref, vg_ref, corpus_ref, mixture_ref, count_ref, seq_ref, dest_ref,
    xs, xr, mixs, mixr, nf, a3, ap, vgr, vgp, wf, acc, ng,
    msf, mp, msd, msc, mrf, mrd, mrc, mown, mxs, mxr, mx, mzs, mzr, ags, agr, gs, gx, gz, gq, st, sty, stx, stz, stc,
    vg_s, vg_r, x_s, x_r, mix_s, mix_r, w_s, w_r, w_r2, ap_s, vgp_s, my_s, my_r, mx_s, mx_r, mz_s, mz_r,
    az_s, az_r, ag_s, ag_r, gx_s, gx_r, gz_s, gz_r, gq_s, gq_r, sty_s, sty_r, stx_s, stx_r, stz_s, stz_r, stc_s, loc, ig_s,
):
    me = lax.axis_index("dp")
    f = lax.axis_index("fsdp")
    x, zl = me // NZ, me % NZ
    zh, y, c = f // 8, (f // 2) % NY, f % 2
    z = zh * 4 + zl

    def at(x_, z_, y_, c_):
        return (x_ * NZ + z_ % 4, (z_ // 4) * 8 + y_ * 2 + c_)

    partner = (me, zh * 8 + y * 2 + 1 - c)

    moves = [
        pltpu.make_async_copy(src, dst, loc.at[4 + i])
        for i, (src, dst) in enumerate((
            (corpus_hbm, corpus_ref), (mixture_hbm, mixture_ref), (count_hbm, count_ref), (seq_hbm, seq_ref),
            (dest_hbm, dest_ref), (x_hbm, x_ref), (vg_hbm, vg_ref), (w_hbm, w_ref), (gain_hbm, gain_ref),
            (bias_hbm, bias_ref),
        ))
    ]
    for cp in moves:
        cp.start()

    bar = pltpu.get_barrier_semaphore()
    greeted = 0
    for k in range(1, 16):
        other = (me + k) % 16
        for dev in ((other, f), (other, partner[1])):
            pl.semaphore_signal(bar, inc=1, device_id=dev, device_id_type=MESH)
            greeted += 1
    for k in range(1, 8):
        pl.semaphore_signal(bar, inc=1, device_id=(me, zh * 8 + (f + k) % 8), device_id_type=MESH)
        greeted += 1
    for k in range(4):
        pl.semaphore_signal(
            bar, inc=1, device_id=(x * NZ + k, (1 - zh) * 8 + y * 2 + c), device_id_type=MESH
        )
        greeted += 1
    for cp in moves[:6]:
        cp.wait()

    def slot(d):
        chosen, live = jnp.int32(0), jnp.int32(0)
        for j in range(dest_ref.shape[0]):
            hit = (dest_ref[j] == d) & (j < count_ref[0])
            chosen = jnp.where(hit, seq_ref[j], chosen)
            live = jnp.where(hit, 1, live)
        mix = mixture_ref[corpus_ref[chosen]] * live
        return chosen, live, mix.astype(F32)

    def gather(d, carry):
        total, number = carry
        chosen, live, mix = slot(d)
        xs[d] = x_ref[chosen]
        mixs[d] = jnp.broadcast_to(mix, (1, 128))
        return total + mix, number + live.astype(F32)

    kept_total, kept_number = lax.fori_loop(0, 16, gather, (jnp.float32(0), jnp.float32(0)))

    for cp in moves[6:]:
        cp.wait()
    pl.semaphore_wait(bar, greeted)

    def vg_put(k):
        d = (me + k) % 16
        return put(vg_ref.at[d], vgr.at[me], vg_s.at[0], vg_r.at[0], (d, f))

    def mix_put(k):
        d = (me + k) % 16
        return put(mixs.at[d], mixr.at[me], mix_s.at[0], mix_r.at[0], (d, f))

    def other_dp(dx, m):
        z_ = zl + m - 2 * ((zl % 2) * (m % 2) + (zl // 2) * (m // 2) * 2)
        return (x + dx) % 4 * NZ + z_

    def x_put(dx, m):
        d = other_dp(dx, m)
        return put(xs.at[d], xr.at[me], x_s.at[0], x_r.at[me], (d, f))

    def w_put(slot_, sem, dev, own=False):
        return put(w_ref if own else wf.at[slot_], wf.at[slot_], w_s.at[sem], w_r.at[slot_], dev)

    def w_half(slot_, half, sem, dev):
        rows = wf.at[slot_, pl.ds(half * (SH // 2), SH // 2)]
        return put(rows, rows, w_s.at[sem], (w_r2 if half else w_r).at[slot_], dev)

    def each(start, stop, fn):
        def step(i, carry):
            fn(i)
            return carry

        lax.fori_loop(start, stop, step, 0)

    y_up, y_down = at(x, z, (y + 1) % 4, c), at(x, z, (y + 3) % 4, c)
    each(1, 16, lambda k: vg_put(k).start())
    edge = (zl == 0) | (zl == 3)
    far = (1 - zh) * 4 + jnp.where(zl == 0, 3, 0)
    near = (1 - zh) * 4 + jnp.where(zl == 0, 2, 1)

    @pl.when(edge)
    def _():
        w_put(f, 1, at(x, far, y, c), True).start()
        w_put(f, 1, at(x, near, y, c), True).start()

    w_put(f, 0, y_up, True).start()
    w_put(f, 0, y_down, True).start()
    w_put(f, 0, partner, True).start()
    each(1, 16, lambda k: mix_put(k).start())

    across = tuple(((1 + i // 2) % 4, 2 + i % 2) for i in range(8))
    beside = ((1, 1), (2, 1), (3, 1), (0, 1))
    along_x = ((1, 0), (3, 0), (2, 0))
    both_axes = ((1, 1), (3, 3), (2, 2), (1, 3), (3, 1), (2, 1), (1, 2), (3, 2), (2, 3))

    def x_go(pairs):
        for dx, m in pairs:
            x_put(dx, m).start()

    own_w = pltpu.make_async_copy(w_ref, wf.at[f], loc.at[0])
    own_x = pltpu.make_async_copy(xs.at[me], xr.at[me], loc.at[1])
    own_vg = pltpu.make_async_copy(vg_ref.at[me], vgr.at[me], loc.at[2])
    own_mix = pltpu.make_async_copy(mixs.at[me], mixr.at[me], loc.at[3])
    for cp in (own_w, own_x, own_vg, own_mix):
        cp.start()

    x_go(both_axes[:7] + along_x)
    def norm(i):
        total = jnp.zeros((TOK, 128), F32)
        for q in range(Q):
            part = x_ref[i, :, q * QW : (q + 1) * QW].astype(F32)
            part = part * part
            for b in range(QW // 128):
                total = total + part[:, b * 128 : (b + 1) * 128]
        inverse = lax.rsqrt(jnp.sum(total, axis=1, keepdims=True) / D + EPSILON)
        for q in range(Q):
            cols = slice(q * QW, (q + 1) * QW)
            nf[i, :, cols] = (x_ref[i, :, cols].astype(F32) * inverse * gain_ref[:, cols]).astype(BF16)

    each(0, 16, norm)

    def kept(d):
        chosen, _, _ = slot(d)
        for q in range(Q):
            a3[q, d] = nf[chosen, :, q * QW : (q + 1) * QW]

    each(0, 16, kept)
    ap_put = put(a3.at[pl.ds((1 - c) * 4, 4)], ap, ap_s.at[0], ap_s.at[1], partner)
    ap_put.start()

    own_vg.wait()
    all_vg = put(vg_ref.at[pl.ds(0, 15)], vgr.at[pl.ds(0, 15)], vg_s.at[0], vg_r.at[0], partner)
    all_vg.wait_recv()
    all_mix = put(mixs.at[pl.ds(0, 15)], mixr.at[pl.ds(0, 15)], mix_s.at[0], mix_r.at[0], partner)

    sa, sb, sf = (zh * 8 + ((y + k) % 4) * 2 + c for k in (1, 3, 2))
    w_in = lambda slot_: put(w_ref, wf.at[slot_], w_s.at[0], w_r.at[slot_], partner)
    w_in(sb).wait_recv()
    w_half(sb, 0, 0, y_up).start()
    w_in(sa).wait_recv()
    w_half(sa, 1, 0, y_down).start()
    w_put(sa, 0, partner).start()
    w_put(sb, 0, partner).start()

    def add_bias(d, total):
        rows = vgr[d].astype(F32) * mixs[d][:, :1]
        vgr[d] = rows.astype(BF16)
        return total + rows

    bias_rows = lax.fori_loop(0, 16, add_bias, jnp.zeros((TOK, V), F32))
    vgp_put = put(vgr, vgp, vgp_s.at[0], vgp_s.at[1], partner)
    vgp_put.start()
    lane = lax.broadcasted_iota(jnp.int32, (1, 128), 1)
    tail = jnp.where(lane == 0, kept_total, jnp.where(lane == 1, kept_number, 0.0))
    mine = jnp.concatenate([jnp.sum(bias_rows, axis=0, keepdims=True), tail], axis=1)
    st[0] = mine
    sty[y] = mine
    st_y = [put(st.at[0], sty.at[y], sty_s.at[0], sty_r.at[0], at(x, z, (y + k) % 4, c)) for k in (1, 2, 3)]
    for cp in st_y:
        cp.start()

    ap_put.wait_recv()
    vgp_put.wait_recv()

    def share(yq, store):
        for b in range(QW // 128):
            cols = slice(b * 128, (b + 1) * 128)
            both = (((0,), (0,)), ((), ()))
            left = a3[c * 4 + yq, :, :, cols].reshape(16 * TOK, 128)
            right = ap[yq, :, :, cols].reshape(16 * TOK, 128)
            part = lax.dot_general(left, vgr[...].reshape(16 * TOK, V), both, preferred_element_type=F32)
            part += lax.dot_general(right, vgp[...].reshape(16 * TOK, V), both, preferred_element_type=F32)
            store(cols, part)

    def to_far(cols, part):
        msf[cols, :] = part.astype(BF16)

    def m_put(kind, way, src, dst):
        return put(src, dst, my_s.at[0], my_r.at[kind * 2 + way], y_down if way else y_up)

    half = SH
    m_far = lambda way: m_put(0, way, msf.at[pl.ds(way * half, half)], mrf.at[way])
    m_near = lambda way: m_put(1, way, msd.at[way], mrd.at[way])
    m_both = lambda way: m_put(2, way, msc.at[way], mrc.at[way])
    share((y + 2) % 4, to_far)
    for way in (0, 1):
        m_far(way).start()
    for way, k in ((0, 1), (1, 3)):
        def to_part(cols, part, way=way):
            mp[way, cols, :] = part

        share((y + k) % 4, to_part)
        msd[way] = mp[way, (1 - way) * half : (2 - way) * half, :].astype(BF16)
        m_near(way).start()

    def to_own(cols, part):
        mown[cols, :] = part

    share(y, to_own)

    for h in (0, 1):
        w_half(sf, h, 0, partner).wait_recv()
    w_put(sf, 0, partner).start()

    all_y = put(sty.at[pl.ds(0, 3)], sty.at[pl.ds(0, 3)], sty_s.at[0], sty_r.at[0], partner)
    all_y.wait_recv()
    mine = ((sty[0] + sty[1]) + sty[2]) + sty[3]
    st[1] = mine
    stx[x] = mine
    st_x = [put(st.at[1], stx.at[x], stx_s.at[0], stx_r.at[0], at((x + k) % 4, z, y, c)) for k in (1, 2, 3)]
    for cp in st_x:
        cp.start()

    own_w.wait()
    acc[...] = jnp.zeros_like(acc)
    vg_all = vg_ref

    def block(q):
        rows = wf[pl.ds(q * 2, 2)].reshape(QW, V)
        acc[...] += jnp.dot(nf[:, :, lanes(q)].reshape(16 * TOK, QW), rows, preferred_element_type=F32)
        grad = lax.dot_general(
            vg_all[...].reshape(16 * TOK, V), rows, (((1,), (1,)), ((), ())), preferred_element_type=F32
        )
        ng[:, :, lanes(q)] = grad.reshape(16, TOK, QW)

    def first_blocks(k):
        yq = (y + k) % 4
        w_in(zh * 8 + yq * 2 + 1 - c).wait_recv()
        block(zh * 4 + yq)

    each(0, 4, first_blocks)

    for way in (0, 1):
        m_far(way).wait_recv()
        msc[way] = (mp[way, way * half : (way + 1) * half, :] + mrf[way].astype(F32)).astype(BF16)
        m_both(way).start()

    oz = (1 - zh) * 8 + c
    w_in(oz + y * 2).wait_recv()
    w_put(oz + y * 2, 0, y_up).start()
    w_put(oz + y * 2, 0, y_down).start()
    w_put(oz + y * 2, 0, partner).start()
    w_in((1 - zh) * 8 + y * 2 + 1 - c).wait_recv()
    block((1 - zh) * 4 + y)

    all_x = put(stx.at[pl.ds(0, 3)], stx.at[pl.ds(0, 3)], stx_s.at[0], stx_r.at[0], partner)
    all_x.wait_recv()
    mine = ((stx[0] + stx[1]) + stx[2]) + stx[3]
    st[2] = mine
    stz[z] = mine
    st_z = [put(st.at[2], stz.at[z], stz_s.at[0], stz_r.at[0], at(x, (z + k) % 8, y, c)) for k in range(1, 8)]
    for cp in st_z:
        cp.start()

    x_go(both_axes[7:])

    for way in (0, 1):
        m_near(way).wait_recv()
        m_both(way).wait_recv()
    for way in (0, 1):
        rows = slice(way * half, (way + 1) * half)
        total = mown[rows, :] + mrc[way].astype(F32) + mrd[1 - way].astype(F32)
        mown[rows, :] = total
        mxs[rows, :] = total.astype(BF16)
    m_x = []
    for k in (2, 1, 3):
        xq = (x + k) % 4
        cp = put(
            mxs.at[pl.ds(pl.multiple_of(xq * 160, 32), 160)], mxr.at[k - 1], mx_s.at[0], mx_r.at[0], at(xq, z, y, c)
        )
        cp.start()
        m_x.append(cp)

    x_go(((0, 2),))

    ta, tb, tf = (oz + ((y + k) % 4) * 2 for k in (1, 3, 2))
    w_in(tb).wait_recv()
    w_half(tb, 0, 0, y_up).start()
    w_in(ta).wait_recv()
    w_half(ta, 1, 0, y_down).start()
    w_put(ta, 0, partner).start()
    w_put(tb, 0, partner).start()

    part = []
    for b in range(2):
        rows = mown[b * SH : (b + 1) * SH, :] * wf[(c * 4 + y) * 2 + b].astype(F32)
        part.append(rows[:, :128] + rows[:, 128:256] + rows[:, 256:384] + rows[:, 384:])
    gains = lax.dot_general(
        jnp.ones((8, 128), F32), jnp.concatenate(part, axis=0), (((1,), (1,)), ((), ())),
        precision=lax.Precision.HIGHEST, preferred_element_type=F32,
    )[:1]
    gs[0] = gains
    gx[x] = gains
    g_x = [put(gs.at[0], gx.at[x], gx_s.at[0], gx_r.at[0], at((x + k) % 4, z, y, c)) for k in (1, 2, 3)]
    for cp in g_x:
        cp.start()

    all_mx = put(mxr, mxr, mx_s.at[0], mx_r.at[0], partner)
    all_mx.wait_recv()
    mx[...] = (
        mown[pl.ds(pl.multiple_of(x * 160, 32), 160), :]
        + mxr[0].astype(F32) + mxr[1].astype(F32) + mxr[2].astype(F32)
    )
    for b in range(4):
        mzs[b] = mx[b * 40 : (b + 1) * 40, :].astype(BF16)

    def z_put(k):
        zq = (z + k) % 8
        return put(mzs.at[zq % 4], mzr.at[z], mz_s.at[0], mz_r.at[0], at(x, zq, y, c))

    for k in range(1, 8):
        @pl.when((z + k) % 8 // 4 == c)
        def _(k=k):
            z_put(k).start()

    all_gx = put(gx.at[pl.ds(0, 3)], gx.at[pl.ds(0, 3)], gx_s.at[0], gx_r.at[0], partner)
    all_gx.wait_recv()
    gains = ((gx[0] + gx[1]) + gx[2]) + gx[3]
    gs[1] = gains
    gz[z] = gains
    g_z = [put(gs.at[1], gz.at[z], gz_s.at[0], gz_r.at[0], at(x, (z + k) % 8, y, c)) for k in range(1, 8)]
    for cp in g_z:
        cp.start()

    for h in (0, 1):
        w_half(tf, h, 0, partner).wait_recv()
    w_put(tf, 0, partner).start()

    def last_blocks(k):
        yq = (y + k + k // 2 + 2 * (k // 3)) % 4
        w_in((1 - zh) * 8 + yq * 2 + 1 - c).wait_recv()
        block((1 - zh) * 4 + yq)

    each(1, 4, last_blocks)
    values_ref[...] = (acc[...] + bias_ref[...]).astype(BF16)
    values_copy = pltpu.make_async_copy(values_ref, values_out, loc.at[14])
    values_copy.start()

    all_z = put(stz.at[pl.ds(0, 7)], stz.at[pl.ds(0, 7)], stz_s.at[0], stz_r.at[0], partner)
    all_z.wait_recv()
    total = stz[0]
    for b in range(1, 8):
        total = total + stz[b]
    st[3] = total
    st_c = put(st.at[3], stc, stc_s.at[0], stc_s.at[1], partner)
    st_c.start()

    sums_here = zh == c
    to_core = x // 2

    def az_put(k):
        return put(ags.at[zl], ags.at[zl], az_s.at[0], az_r.at[0], at(x, zh * 4 + (zl + k) % 4, y, c))

    @pl.when(sums_here)
    def _():
        mzr[z] = mzs[zl]
        put(mzr.at[pl.ds(0, 7)], mzr.at[pl.ds(0, 7)], mz_s.at[0], mz_r.at[0], partner).wait_recv()
        total = mzr[0].astype(F32)
        for b in range(1, 8):
            total += mzr[b].astype(F32)
        ags[zl] = total.astype(BF16)
        for k in (2, 1, 3):
            az_put(k).start()

    x_go(((0, 3), (0, 1)))

    all_gz = put(gz.at[pl.ds(0, 7)], gz.at[pl.ds(0, 7)], gz_s.at[0], gz_r.at[0], partner)
    all_gz.wait_recv()
    gains = gz[0]
    for b in range(1, 8):
        gains = gains + gz[b]
    gs[2] = gains
    mine_q = c * 4 + y
    gq[mine_q] = gains
    g_q = []
    for k in range(1, 8):
        cp = put(gs.at[2], gq.at[mine_q], gq_s.at[0], gq_r.at[0], (me, zh * 8 + (f + k) % 8))
        cp.start()
        g_q.append(cp)

    st_c.wait_recv()
    total = st[3] + stc[...]
    ratio = total[:, V + 1 : V + 2] / total[:, V : V + 1]
    bgrad_ref[...] = total[:, :V] * ratio

    own_x.wait()
    own_mix.wait()
    all_mix.wait_recv()

    def slot_copy(s):
        return pltpu.make_async_copy(igrad_ref.at[s], igrad_out.at[s], ig_s.at[0])

    def slot_grad(s):
        squares = jnp.zeros((TOK, 128), F32)
        products = jnp.zeros((TOK, 128), F32)
        for q in range(Q):
            cols = slice(q * QW, (q + 1) * QW)
            rows = xr[s, :, cols].astype(F32)
            both = ng[s, :, cols] * gain_ref[:, cols] * rows
            rows = rows * rows
            for b in range(QW // 128):
                squares = squares + rows[:, b * 128 : (b + 1) * 128]
                products = products + both[:, b * 128 : (b + 1) * 128]
        inverse = lax.rsqrt(jnp.sum(squares, axis=1, keepdims=True) / D + EPSILON)
        mean = jnp.sum(products, axis=1, keepdims=True) / D
        scale = ratio * mixr[s][:, :1]
        left = inverse * scale
        right = inverse * inverse * inverse * mean * scale
        for q in range(Q):
            cols = slice(q * QW, (q + 1) * QW)
            rows = xr[s, :, cols].astype(F32)
            igrad_ref[s, :, cols] = (left * (ng[s, :, cols] * gain_ref[:, cols]) - rows * right).astype(BF16)
        slot_copy(s).start()

    slot_grad(me)

    def take(dx, m):
        s = other_dp(4 - dx, m)
        put(xs.at[0], xr.at[s], x_s.at[0], x_r.at[s], partner).wait_recv()
        slot_grad(s)

    each(1, 4, lambda i: take(i, 0))
    each(0, 5, lambda i: take((1 + i // 2) % 4, 2 + i % 2))

    @pl.when(sums_here)
    def _():
        put(mzr.at[pl.ds(0, 3)], ags.at[pl.ds(0, 3)], az_s.at[0], az_r.at[0], partner).wait_recv()
        for k in (2, 1, 3):
            put(ags, agr.at[x % 2], ag_s.at[k - 1], ag_r.at[x % 2], at((x + k) % 4, z, y, to_core)).start()

        @pl.when(to_core == c)
        def _():
            agr[x % 2] = ags[...]

        @pl.when(to_core != c)
        def _():
            put(ags, agr.at[x % 2], ag_s.at[3], ag_r.at[x % 2], partner).start()

    each(5, 8, lambda i: take((1 + i // 2) % 4, 2 + i % 2))
    each(1, 5, lambda i: take(i % 4, 1))

    for b in range(2):
        here = sums_here & (to_core == c) & (x % 2 == b)

        @pl.when(jnp.logical_not(here))
        def _(b=b):
            put(agr.at[b], agr.at[b], ag_s.at[0], ag_r.at[b], partner).wait_recv()

    for b in range(2):
        for k in range(4):
            wgrad_ref[(b * 4 + k) * 40 : (b * 4 + k + 1) * 40, :] = agr[b, k].astype(F32) * ratio
    wgrad_copy = pltpu.make_async_copy(wgrad_ref, wgrad_out, loc.at[15])
    wgrad_copy.start()

    all_gq = put(gq.at[pl.ds(0, 7)], gq.at[pl.ds(0, 7)], gq_s.at[0], gq_r.at[0], partner)
    all_gq.wait_recv()
    for q in range(Q):
        cols = slice(q * QW, (q + 1) * QW)
        ggrad_ref[:, cols] = gq[q] * ratio / gain_ref[:, cols]

    values_copy.wait()
    wgrad_copy.wait()
    pltpu.make_async_copy(igrad_ref, igrad_out, ig_s.at[0]).wait()
    all_vg.wait_send()
    all_mix.wait_send()
    put(xs.at[pl.ds(0, 15)], xr.at[pl.ds(0, 15)], x_s.at[0], x_r.at[0], partner).wait_send()

    @pl.when(edge)
    def _():
        put(wf.at[pl.ds(0, 2)], wf.at[pl.ds(0, 2)], w_s.at[1], w_r.at[0], partner).wait_send()

    put(wf.at[pl.ds(0, 14)], wf.at[pl.ds(0, 14)], w_s.at[0], w_r.at[0], partner).wait_send()
    put(wf.at[pl.ds(0, 6)], wf.at[pl.ds(0, 6)], my_s.at[0], w_r.at[0], partner).wait_send()
    for cp in (ap_put, vgp_put, st_c, all_y, all_x, all_z, all_gx, all_gz, all_gq, all_mx):
        cp.wait_send()
    @pl.when(sums_here)
    def _():
        put(mzs.at[pl.ds(0, 3)], mzr.at[pl.ds(0, 3)], mz_s.at[0], mz_r.at[0], partner).wait_send()
        put(mzr.at[pl.ds(0, 3)], mzr.at[pl.ds(0, 3)], az_s.at[0], az_r.at[0], partner).wait_send()
        put(agr.at[0], agr.at[0], ag_s.at[0], ag_r.at[0], partner).wait_send()
        put(agr.at[0], agr.at[0], ag_s.at[1], ag_r.at[0], partner).wait_send()
        put(agr.at[0], agr.at[0], ag_s.at[2], ag_r.at[0], partner).wait_send()

        @pl.when(to_core != c)
        def _():
            put(agr.at[0], agr.at[0], ag_s.at[3], ag_r.at[0], partner).wait_send()

    @pl.when(jnp.logical_not(sums_here))
    def _():
        put(mzs, mzs, mz_s.at[0], mz_r.at[0], partner).wait_send()


def body(
    layer_in, norm_gain, v_weight, v_bias, corpus, mixture, keep_count, keep_seq, keep_dest, value_grad
):
    vmem = pl.BlockSpec(memory_space=pltpu.VMEM)
    hbm = pl.BlockSpec(memory_space=pltpu.HBM)
    smem = pltpu.SMEM
    dma = pltpu.SemaphoreType.DMA
    values, input_grad, weight_grad, gain_grad, bias_grad = pl.pallas_call(
        kernel,
        out_shape=(
            pltpu.VMEM((16 * TOK, V), BF16),
            pltpu.VMEM((16, TOK, D), BF16),
            pltpu.VMEM((SH, V), F32),
            pltpu.VMEM((1, D), F32),
            pltpu.VMEM((1, V), F32),
        ),
        in_specs=[hbm] * 10,
        out_specs=[pl.BlockSpec(memory_space=pl.ANY)] * 3 + [vmem] * 2,
        scratch_shapes=[
            pltpu.VMEM((16 * TOK, V), BF16), pltpu.VMEM((16, TOK, D), BF16), pltpu.VMEM((SH, V), F32),
            pltpu.VMEM((16, TOK, D), BF16), pltpu.VMEM((1, D), F32), pltpu.VMEM((SH, V), BF16),
            pltpu.VMEM((1, V), F32), pltpu.VMEM((16, TOK, V), BF16),
            smem(corpus.shape, jnp.int32), smem(mixture.shape, jnp.int32), smem((1,), jnp.int32),
            smem(keep_seq.shape[2:], jnp.int32), smem(keep_dest.shape[2:], jnp.int32),
            pltpu.VMEM((16, TOK, D), BF16),
            pltpu.VMEM((16, TOK, D), BF16),
            pltpu.VMEM((16, 1, 128), F32),
            pltpu.VMEM((16, 1, 128), F32),
            pltpu.VMEM((16, TOK, D), BF16),
            pltpu.VMEM((Q, 16, TOK, QW), BF16),
            pltpu.VMEM((4, 16, TOK, QW), BF16),
            pltpu.VMEM((16, TOK, V), BF16),
            pltpu.VMEM((16, TOK, V), BF16),
            pltpu.VMEM((NF, SH, V), BF16),
            pltpu.VMEM((16 * TOK, V), F32),
            pltpu.VMEM((16, TOK, D), F32),
            pltpu.VMEM((QW, V), BF16),
            pltpu.VMEM((2, QW, V), F32),
            pltpu.VMEM((2, SH, V), BF16),
            pltpu.VMEM((2, SH, V), BF16),
            pltpu.VMEM((2, SH, V), BF16),
            pltpu.VMEM((2, SH, V), BF16),
            pltpu.VMEM((2, SH, V), BF16),
            pltpu.VMEM((QW, V), F32),
            pltpu.VMEM((QW, V), BF16),
            pltpu.VMEM((3, QW // 4, V), BF16),
            pltpu.VMEM((QW // 4, V), F32),
            pltpu.VMEM((4, QW // 16, V), BF16),
            pltpu.VMEM((8, QW // 16, V), BF16),
            pltpu.VMEM((4, QW // 16, V), BF16),
            pltpu.VMEM((2, 4, QW // 16, V), BF16),
            pltpu.VMEM((3, 1, QW), F32),
            pltpu.VMEM((4, 1, QW), F32),
            pltpu.VMEM((8, 1, QW), F32),
            pltpu.VMEM((Q, 1, QW), F32),
            pltpu.VMEM((4, 1, V + 128), F32),
            pltpu.VMEM((4, 1, V + 128), F32),
            pltpu.VMEM((4, 1, V + 128), F32),
            pltpu.VMEM((8, 1, V + 128), F32),
            pltpu.VMEM((1, V + 128), F32),
            dma((1,)), dma((1,)), dma((1,)), dma((16,)), dma((1,)), dma((1,)),
            dma((2,)), dma((16,)), dma((16,)), dma((2,)), dma((2,)),
            dma((1,)), dma((6,)), dma((1,)), dma((1,)), dma((1,)), dma((1,)),
            dma((1,)), dma((1,)), dma((4,)), dma((2,)),
            dma((1,)), dma((1,)), dma((1,)), dma((1,)), dma((1,)), dma((1,)),
            dma((1,)), dma((1,)), dma((1,)), dma((1,)), dma((1,)), dma((1,)), dma((2,)), dma((16,)), dma((1,)),
        ],
        compiler_params=pltpu.CompilerParams(
            collective_id=0, has_side_effects=True, vmem_limit_bytes=57 * 1024 * 1024
        ),
        name="step",
    )(
        layer_in, norm_gain[None, :], v_weight, v_bias[None, :], value_grad[0, 0],
        corpus, mixture, keep_count[0], keep_seq[0, 0], keep_dest[0, 0],
    )
    return (
        values.reshape(16, TOK, V), input_grad[None, None], weight_grad, gain_grad[0], bias_grad[0],
    )


def solution(mesh):
    return jax.shard_map(
        body,
        mesh=mesh,
        in_specs=(
            P(("dp", "fsdp"), None, None),
            P(),
            P("fsdp", None),
            P(),
            P(("dp", "fsdp")),
            P(),
            P("dp", "fsdp"),
            P("dp", "fsdp", None),
            P("dp", "fsdp", None),
            P("dp", "fsdp", None, None, None),
        ),
        out_specs=(
            P(("dp", "fsdp"), None, None),
            P("dp", "fsdp", None, None, None),
            P("fsdp", None),
            P(),
            P(),
        ),
        check_vma=False,
    )
```
